32 devices in a mesh: dp: 4 (over z), seq: 4 (over y, x), tensor: 2 (over core).
Axes of the slice: x: 2, y: 2, z: 4, core: 2. Of those that a mesh axis runs over, the one named last changes fastest.
Arguments:
- tokens: bfloat16 [8, 4, 256, 1152], P('dp', 'seq'), may hold values from -6 to 6
- conditioning: float32 [8, 1152], P(None, ('dp', 'seq', 'tensor')), may hold values from -5 to 5
- cotangent: bfloat16 [8, 4, 256, 1152], P('dp', 'seq'), may hold values from -6 to 6
- modulation_weight: bfloat16 [2, 1152, 6912], P(None, ('dp', 'seq', 'tensor')), may hold values from -0.25 to 0.25
- modulation_bias: bfloat16 [2, 6912], P(None, ('dp', 'seq', 'tensor')), may hold values from -2 to 2
- triple_weight: bfloat16 [2, 1152, 3, 1152], P(None, ('dp', 'seq'), None, 'tensor'), may hold values from -0.1875 to 0.1875
- pair_bias: bfloat16 [2, 2, 2, 576], P(None, None, 'tensor', ('dp', 'seq')), may hold values from -3 to 3
- out_weight: bfloat16 [2, 1152, 1152], P(None, 'tensor', ('dp', 'seq')), may hold values from -1 to 1
- out_bias: bfloat16 [2, 1152], P(None, ('dp', 'seq')), may hold values from -2 to 2
- hidden_weight: bfloat16 [2, 1152, 4608], P(None, ('dp', 'seq'), 'tensor'), may hold values from -0.1875 to 0.1875
- hidden_bias: bfloat16 [2, 2, 2304], P(None, 'tensor', ('dp', 'seq')), may hold values from -3 to 3
- output_weight: bfloat16 [2, 4608, 1152], P(None, 'tensor', ('dp', 'seq')), may hold values from -0.09375 to 0.09375
- output_bias: bfloat16 [2, 1152], P(None, ('dp', 'seq')), may hold values from -2 to 2
Outputs:
- activations: bfloat16 [8, 4, 256, 1152], P('dp', 'seq')
- input_grad: float32 [8, 4, 256, 1152], P('dp', 'seq')
- cond_grad: float32 [8, 1152], P(None, ('dp', 'seq', 'tensor'))
- modulation_weight_grad: float32 [2, 1152, 6912], P(None, ('dp', 'seq', 'tensor'))
- modulation_bias_grad: float32 [2, 6912], P(None, ('dp', 'seq', 'tensor'))
- triple_weight_grad: float32 [2, 1152, 3, 1152], P(None, ('dp', 'seq'), None, 'tensor')
- pair_bias_grad: float32 [2, 2, 2, 576], P(None, None, 'tensor', ('dp', 'seq'))
- out_weight_grad: float32 [2, 1152, 1152], P(None, 'tensor', ('dp', 'seq'))
- out_bias_grad: float32 [2, 1152], P(None, ('dp', 'seq'))
- hidden_weight_grad: float32 [2, 1152, 4608], P(None, ('dp', 'seq'), 'tensor')
- hidden_bias_grad: float32 [2, 2, 2304], P(None, 'tensor', ('dp', 'seq'))
- output_weight_grad: float32 [2, 4608, 1152], P(None, 'tensor', ('dp', 'seq'))
- output_bias_grad: float32 [2, 1152], P(None, ('dp', 'seq'))
The draws below stay inside these ranges and needn't reach their ends.
All inputs are finite; a program needn't handle non-finite values.
Results may differ from the reference program's by a relative error of at most 0.028.
Values may be sent and summed in bfloat16 or wider, within the bound.
No kernel may reach another device: no remote copies, remote signals or barrier semaphores. Data moves between devices by JAX's collectives and lax.ppermute only.
A program may use at most 320 MiB of HBM per device.

```python
import jax
import jax.numpy as jnp
from jax import lax

D = 1152
HEADS = 16
HEAD_DIM = 72
FF = 4608
PATCHES = 256
LAYERS = 2
FRAMES = 4
CLIPS = 8
N_TENSOR = 2


def shard_levels(rng, dims, cuts, least, top_value):
    factor_of, own = 1.0, jax.random.fold_in(rng, 6)
    for dim, shards_of in cuts:
        heights = jnp.exp(jax.random.uniform(jax.random.fold_in(own, dim), (shards_of,), jnp.float32, least / len(cuts), top_value / len(cuts)))
        factor_of = factor_of * jnp.repeat(heights, dims[dim] // shards_of).reshape([-1 if axis == dim else 1 for axis in range(len(dims))])
    return factor_of


def normal_values(own_key, extent, width, most, cuts=(), kind=jnp.bfloat16):
    gain = shard_levels(own_key, extent, cuts, -0.22, 0.18) if cuts else 1.0
    drawn = jax.random.normal(own_key, extent, jnp.float32) * width * gain
    return jnp.minimum(jnp.maximum(drawn, -most), most).astype(kind)


def setup_inputs(seed: int = 0) -> dict:
    seeds = jax.random.split(jax.random.key(seed), 14)
    tokens = normal_values(seeds[0], (CLIPS, FRAMES, PATCHES, D), 1.0, 6.0, ((0, 4), (1, 4)))
    conditioning = normal_values(seeds[1], (CLIPS, D), 1.0, 5.0, ((1, 32),), jnp.float32)
    cotangent = normal_values(seeds[2], (CLIPS, FRAMES, PATCHES, D), 1.0, 6.0, ((0, 4), (1, 4)))
    modulation_weight = normal_values(seeds[3], (LAYERS, D, 6 * D), (D // 2) ** -0.5, 0.25, ((1, 32),))
    modulation_bias = normal_values(seeds[4], (LAYERS, 6 * D), 0.3, 2.0, ((1, 32),))
    triple_weight = normal_values(seeds[5], (LAYERS, D, 3, D), D ** -0.5, 0.1875, ((1, 16), (3, 2)))
    pair_bias = normal_values(seeds[6], (LAYERS, 2, N_TENSOR, D // N_TENSOR), 0.5, 3.0, ((2, 2), (3, 16)))
    out_weight = normal_values(seeds[7], (LAYERS, D, D), (D // 32) ** -0.5, 1.0, ((1, 2), (2, 16)))
    out_bias = normal_values(seeds[8], (LAYERS, D), 0.3, 2.0, ((1, 16),))
    hidden_weight = normal_values(seeds[9], (LAYERS, D, FF), D ** -0.5, 0.1875, ((1, 16), (2, 2)))
    hidden_bias = normal_values(seeds[10], (LAYERS, N_TENSOR, FF // N_TENSOR), 0.5, 3.0, ((1, 2), (2, 16)))
    output_weight = normal_values(seeds[11], (LAYERS, FF, D), FF ** -0.5, 0.09375, ((1, 2), (2, 16)))
    output_bias = normal_values(seeds[12], (LAYERS, D), 0.3, 2.0, ((1, 16),))
    return {"tokens": tokens, "conditioning": conditioning, "cotangent": cotangent, "modulation_weight": modulation_weight, "modulation_bias": modulation_bias, "triple_weight": triple_weight, "pair_bias": pair_bias, "out_weight": out_weight, "out_bias": out_bias, "hidden_weight": hidden_weight, "hidden_bias": hidden_bias, "output_weight": output_weight, "output_bias": output_bias}


epsilon = 1e-06
highest = lax.Precision.HIGHEST

@jax.custom_vjp
def low(v):
    return lax.optimization_barrier(v.astype(jnp.bfloat16)).astype(jnp.float32)

@jax.custom_vjp
def low_back(v):
    return v

def low_keep(v):
    return (low(v), None)

def low_pass(kept, grad):
    return (grad,)

def back_keep(v):
    return (v, None)

def back_low(kept, grad):
    return (low(grad),)
low.defvjp(low_keep, low_pass)
low_back.defvjp(back_keep, back_low)

def normalize(values):
    average = lax.optimization_barrier(jnp.mean(values, axis=-1, keepdims=True))
    centered = values - average
    variance = lax.optimization_barrier(jnp.mean(centered * centered, axis=-1, keepdims=True))
    return centered * lax.rsqrt(variance + epsilon)

def softmax_rows(scores):
    highest_score = lax.optimization_barrier(jnp.max(scores, axis=-1, keepdims=True))
    weights = jnp.exp(scores - highest_score)
    return weights / lax.optimization_barrier(jnp.sum(weights, axis=-1, keepdims=True))

def spatial_frame(items):
    queries, key_rows, value_rows = items
    factor = HEAD_DIM ** (-0.5)
    scores = low_back(jnp.einsum('phe,qhe->hpq', queries, key_rows, precision=highest) * factor)
    probability = low(softmax_rows(scores))
    return jnp.einsum('hpq,qhe->phe', probability, value_rows, precision=highest)

def temporal_clip(queries, key_rows, value_rows):
    factor = HEAD_DIM ** (-0.5)
    scores = low_back(jnp.einsum('fphe,gphe->phfg', queries, key_rows, precision=highest) * factor)
    probability = low(softmax_rows(scores))
    return jnp.einsum('phfg,gphe->fphe', probability, value_rows, precision=highest)

def modulation(conditioning, modulation_weight, modulation_bias):
    act_cond = low(jax.nn.silu(conditioning))
    return low_back(jnp.einsum('cd,lde->cle', act_cond, modulation_weight, precision=highest) + modulation_bias[None])

def clip_forward(params, mod_clip, residual):
    triple_weight, pair_bias, out_weight, out_bias, hidden_weight, hidden_bias, output_weight, output_bias = params
    frames, patches = (residual.shape[0], residual.shape[1])
    for layer_idx in range(LAYERS):
        mod_rows = mod_clip[layer_idx].reshape(6, D)
        normed_one = low(normalize(residual) * (1.0 + mod_rows[1]) + mod_rows[0])
        biases = pair_bias[layer_idx].reshape(2, D)
        triple_bias = jnp.stack([biases[0], jnp.zeros_like(biases[0]), biases[1]])
        triple = jnp.einsum('fpd,dte->fpte', normed_one, triple_weight[layer_idx], precision=highest) + triple_bias
        triple = low_back(low(triple)).reshape(frames, patches, 3, HEADS, HEAD_DIM)
        queries, key_rows, value_rows = (triple[:, :, 0], triple[:, :, 1], triple[:, :, 2])
        if layer_idx == 0:
            attended = lax.map(jax.checkpoint(spatial_frame), (queries, key_rows, value_rows))
        else:
            attended = temporal_clip(queries, key_rows, value_rows)
        attended = low_back(low(attended.reshape(frames, patches, D)))
        branch = low_back(jnp.einsum('fpe,ed->fpd', attended, out_weight[layer_idx], precision=highest) + out_bias[layer_idx])
        residual = residual + mod_rows[2] * branch
        normed_two = low(normalize(residual) * (1.0 + mod_rows[4]) + mod_rows[3])
        pre_act = low_back(jnp.einsum('fpd,de->fpe', normed_two, hidden_weight[layer_idx], precision=highest) + hidden_bias[layer_idx].reshape(FF))
        hidden = low(jax.nn.gelu(pre_act, approximate=True))
        mlp_out = low_back(jnp.einsum('fpe,ed->fpd', hidden, output_weight[layer_idx], precision=highest) + output_bias[layer_idx])
        residual = residual + mod_rows[5] * mlp_out
    return residual

def reference(tokens, conditioning, cotangent, modulation_weight, modulation_bias, triple_weight, pair_bias, out_weight, out_bias, hidden_weight, hidden_bias, output_weight, output_bias):
    mods, mod_back = jax.vjp(modulation, conditioning.astype(jnp.float32), modulation_weight.astype(jnp.float32), modulation_bias.astype(jnp.float32))
    params = (triple_weight.astype(jnp.float32), pair_bias.astype(jnp.float32), out_weight.astype(jnp.float32), out_bias.astype(jnp.float32), hidden_weight.astype(jnp.float32), hidden_bias.astype(jnp.float32), output_weight.astype(jnp.float32), output_bias.astype(jnp.float32))

    def per_clip(running, inputs):
        residual, grad_out, mod_clip = inputs
        result, clip_back = jax.vjp(clip_forward, params, mod_clip, residual)
        grad_params, grad_mod, grad_in = clip_back(grad_out)
        running = jax.tree.map(lambda first_tree, second_tree: first_tree + second_tree, running, grad_params)
        return (running, (result.astype(jnp.bfloat16), grad_in, grad_mod))
    zero_grads = jax.tree.map(jnp.zeros_like, params)
    summed, outputs = lax.scan(per_clip, zero_grads, (tokens.astype(jnp.float32), cotangent.astype(jnp.float32), mods))
    activations, input_grad, grad_mods = outputs
    cond_grad, modulation_weight_grad, modulation_bias_grad = mod_back(grad_mods)
    return (activations, input_grad, cond_grad, modulation_weight_grad, modulation_bias_grad, summed[0], summed[1], summed[2], summed[3], summed[4], summed[5], summed[6], summed[7])
```

```python
from functools import partial

import jax
import jax.numpy as jnp
from jax import lax
from jax.experimental import pallas as pl
from jax.experimental.pallas import tpu as pltpu
from jax.sharding import PartitionSpec as P

HEAD_DIM = 72
LANES = 128
EPSILON = 1e-06
VMEM_LIMIT = 48 * 1024 * 1024
f32 = jnp.float32
bf16 = jnp.bfloat16


def bits_of(size):
    return max(size.bit_length() - 1, 0)


def pxor(value, axis, flip):
    size = lax.axis_size(axis)
    return lax.ppermute(value, axis, [(i, i ^ flip) for i in range(size)])


def swap(value):
    return pxor(value, "tensor", 1)


def take(value, axis, index):
    return lax.dynamic_index_in_dim(value, index, axis, keepdims=False)


def gather_tree(block, axis, order):
    blocks = {0: block}
    for bit in order:
        for rel in list(blocks):
            blocks[rel | (1 << bit)] = pxor(blocks[rel], axis, 1 << bit)
    return [blocks[rel] for rel in range(len(blocks))]


def place_kernel(idx_ref, *refs):
    blocks, out_ref = refs[:-1], refs[-1]
    for rel, block in enumerate(blocks):
        out_ref[0, jnp.bitwise_xor(idx_ref[1], rel)] = block[0]


def place(blocks, outer_index, inner_index):
    outer, rows, cols = blocks[0].shape
    inner = len(blocks)
    start = jnp.int32(0) if outer_index is None else outer_index
    index = jnp.stack([start, inner_index]).astype(jnp.int32)
    return pl.pallas_call(
        place_kernel,
        grid_spec=pltpu.PrefetchScalarGridSpec(
            num_scalar_prefetch=1,
            grid=(outer,),
            in_specs=[pl.BlockSpec((1, rows, cols), lambda o, idx: (o, 0, 0))] * inner,
            out_specs=pl.BlockSpec(
                (1, inner, rows, cols), lambda o, idx: (jnp.bitwise_xor(idx[0], o), 0, 0, 0)
            ),
        ),
        out_shape=jax.ShapeDtypeStruct((outer, inner, rows, cols), blocks[0].dtype),
        compiler_params=pltpu.CompilerParams(vmem_limit_bytes=VMEM_LIMIT),
        name="place",
    )(index, *blocks)


def finish_gather(halves, dp_index, seq_index):
    count = bits_of(lax.axis_size("seq"))
    whole = []
    for which, half in enumerate(halves):
        order = list(range(count))
        if which % 2:
            order.reverse()
        placed = place(gather_tree(half, "seq", order), dp_index, seq_index)
        whole.append(placed.reshape(-1, half.shape[-1]))
    return whole


def scatter_bits(value, axis, order, first_dim):
    index = lax.axis_index(axis)
    left = list(reversed(range(bits_of(lax.axis_size(axis)))))
    for bit in order:
        dim = first_dim + left.index(bit)
        mine = (index >> bit) & 1
        other = pxor(take(value, dim, 1 - mine), axis, 1 << bit)
        value = (take(value, dim, mine).astype(f32) + other.astype(f32)).astype(value.dtype)
        left.remove(bit)
    return value


def scatter_seq(grad, which):
    parts, clusters = lax.axis_size("seq"), lax.axis_size("dp")
    count = bits_of(parts)
    rows = grad.shape[0] // (parts * clusters)
    order = list(range(count))
    if which % 2 == 0:
        order.reverse()
    view = grad.reshape((clusters,) + (2,) * count + (rows, grad.shape[1]))
    return scatter_bits(view, "seq", order, 1)


def scatter_dp_tree(value):
    count = bits_of(lax.axis_size("dp"))
    view = value.reshape((2,) * count + value.shape[1:])
    return scatter_bits(view, "dp", list(range(count)), 0)


def gather_small(value, axis):
    size, index = lax.axis_size(axis), lax.axis_index(axis)
    out = jnp.zeros((size,) + value.shape, value.dtype)
    for rel in range(size):
        part = value if rel == 0 else pxor(value, axis, rel)
        out = lax.dynamic_update_slice_in_dim(out, part[None], index ^ rel, 0)
    return out


def scatter_small(value, axis):
    size, index = lax.axis_size(axis), lax.axis_index(axis)
    total = take(value, 0, index)
    for rel in range(1, size):
        total = total + pxor(take(value, 0, index ^ rel), axis, rel)
    return total


def sum_small(value, axis):
    total = value
    for rel in range(1, lax.axis_size(axis)):
        total = total + pxor(value, axis, rel)
    return total


def dispatch(rows):
    size, index = lax.axis_size("seq"), lax.axis_index("seq")
    view = rows.reshape(rows.shape[0], size, rows.shape[1] // size, rows.shape[2])
    parts = []
    for rel in range(size):
        part = take(view, 1, index ^ rel)
        parts.append(part if rel == 0 else pxor(part, "seq", rel))
    return jnp.stack(parts, axis=1)


def collect(parts):
    size, index = lax.axis_size("seq"), lax.axis_index("seq")
    blocks = []
    for rel in range(size):
        block = parts[:, rel]
        blocks.append(block if rel == 0 else pxor(block, "seq", rel))
    placed = place(blocks, None, index)
    return placed.reshape(placed.shape[0], -1, placed.shape[-1])


def head_windows(width):
    spans = []
    for first in range(0, width, HEAD_DIM):
        low = first // LANES * LANES
        high = min(-(-(first + HEAD_DIM) // LANES) * LANES, width)
        spans.append((first, low, high))
    return spans


def head_mask(first, low, high):
    lane = lax.broadcasted_iota(jnp.int32, (1, high - low), 1) + low
    return jnp.where((lane >= first) & (lane < first + HEAD_DIM), 1.0, 0.0).astype(bf16)


def row_dot(left, right):
    return lax.dot_general(left, right, (((1,), (1,)), ((), ())), preferred_element_type=f32)


def col_dot(left, right):
    return lax.dot_general(left, right, (((0,), (0,)), ((), ())), preferred_element_type=f32)


def softmax_probs(queries, key_rows, apart):
    scores = row_dot(queries, key_rows) * (HEAD_DIM ** (-0.5))
    if apart is not None:
        scores = jnp.where(apart, -1e30, scores)
    top = jnp.max(scores, axis=-1, keepdims=True)
    weights = jnp.exp(scores - top)
    return weights * (1.0 / jnp.sum(weights, axis=-1, keepdims=True))


def tokens_apart(rows, period):
    if period is None:
        return None
    one = lax.broadcasted_iota(jnp.int32, (rows, rows), 0)
    two = lax.broadcasted_iota(jnp.int32, (rows, rows), 1)
    return lax.rem(one, period) != lax.rem(two, period)


def attend_kernel(period, qk_ref, v_ref, out_ref, acc_ref):
    rows, width = v_ref.shape[1], v_ref.shape[2]
    apart = tokens_apart(rows, period)
    queries, key_rows, value_rows = qk_ref[0, :, :width], qk_ref[0, :, width:], v_ref[0]
    acc_ref[...] = jnp.zeros_like(acc_ref)
    for first, low, high in head_windows(width):
        mask = head_mask(first, low, high)
        probs = softmax_probs(queries[:, low:high] * mask, key_rows[:, low:high], apart)
        acc_ref[:, low:high] += jnp.dot(
            probs.astype(bf16), value_rows[:, low:high] * mask, preferred_element_type=f32
        )
    out_ref[0] = acc_ref[...].astype(bf16)


def attend(qk, values, period):
    blocks, rows, width = values.shape
    return pl.pallas_call(
        partial(attend_kernel, period),
        grid=(blocks,),
        out_shape=jax.ShapeDtypeStruct(values.shape, bf16),
        in_specs=[
            pl.BlockSpec((1, rows, 2 * width), lambda b: (b, 0, 0)),
            pl.BlockSpec((1, rows, width), lambda b: (b, 0, 0)),
        ],
        out_specs=pl.BlockSpec((1, rows, width), lambda b: (b, 0, 0)),
        scratch_shapes=[pltpu.VMEM((rows, width), f32)],
        compiler_params=pltpu.CompilerParams(vmem_limit_bytes=VMEM_LIMIT),
        name="attend",
    )(qk, values)


def attend_grad_kernel(period, qk_ref, v_ref, da_ref, dqk_ref, dv_ref, acc_q, acc_k, acc_v):
    rows, width = v_ref.shape[1], v_ref.shape[2]
    apart = tokens_apart(rows, period)
    queries, key_rows, value_rows = qk_ref[0, :, :width], qk_ref[0, :, width:], v_ref[0]
    grad_att = da_ref[0]
    factor = HEAD_DIM ** (-0.5)
    for acc in (acc_q, acc_k, acc_v):
        acc[...] = jnp.zeros_like(acc)
    for first, low, high in head_windows(width):
        mask = head_mask(first, low, high)
        q_own = queries[:, low:high] * mask
        k_own = key_rows[:, low:high] * mask
        g_own = grad_att[:, low:high] * mask
        probs = softmax_probs(q_own, k_own, apart)
        grad_probs = row_dot(g_own, value_rows[:, low:high])
        inner = jnp.sum(grad_probs * probs, axis=-1, keepdims=True)
        grad_scores = (probs * (grad_probs - inner)).astype(bf16)
        acc_q[:, low:high] += jnp.dot(grad_scores, k_own, preferred_element_type=f32)
        acc_k[:, low:high] += col_dot(grad_scores, q_own)
        acc_v[:, low:high] += col_dot(probs.astype(bf16), g_own)
    dqk_ref[0, :, :width] = (acc_q[...] * factor).astype(bf16)
    dqk_ref[0, :, width:] = (acc_k[...] * factor).astype(bf16)
    dv_ref[0] = acc_v[...].astype(bf16)


def attend_grad(qk, values, grad_att, period):
    blocks, rows, width = values.shape
    wide = pl.BlockSpec((1, rows, 2 * width), lambda b: (b, 0, 0))
    thin = pl.BlockSpec((1, rows, width), lambda b: (b, 0, 0))
    return pl.pallas_call(
        partial(attend_grad_kernel, period),
        grid=(blocks,),
        out_shape=(
            jax.ShapeDtypeStruct(qk.shape, bf16),
            jax.ShapeDtypeStruct(values.shape, bf16),
        ),
        in_specs=[wide, thin, thin],
        out_specs=(wide, thin),
        scratch_shapes=[pltpu.VMEM((rows, width), f32)] * 3,
        compiler_params=pltpu.CompilerParams(vmem_limit_bytes=VMEM_LIMIT),
        name="attend_grad",
    )(qk, values, grad_att)


def normalize(values):
    average = jnp.mean(values, axis=-1, keepdims=True)
    centered = values - average
    variance = jnp.mean(centered * centered, axis=-1, keepdims=True)
    return centered * lax.rsqrt(variance + EPSILON)


def modulate(values, shift_row, scale_row):
    return normalize(values) * (1.0 + scale_row) + shift_row


def both_clips(own):
    return jnp.concatenate([own, swap(own)], axis=0)


def own_total(partial_sum):
    rows = partial_sum.shape[0] // 2
    return partial_sum[:rows] + swap(partial_sum[rows:])


def mm(left, right):
    return jnp.dot(left, right, preferred_element_type=f32)


def layer_forward(x, mods, weights, biases, temporal):
    (w_qk, w_vo), (w_up_a, w_up_b), (w_down_a, w_down_b) = weights
    bias_q, bias_v, bias_out, bias_up, bias_down = biases
    width = bias_q.shape[0]
    half = w_up_a.shape[1]
    patches = x.shape[0]
    normed_one = both_clips(modulate(x, mods[0], mods[1]).astype(bf16))
    qk = (mm(normed_one, w_qk) + jnp.concatenate([bias_q, jnp.zeros_like(bias_q)])).astype(bf16)
    values = (mm(normed_one, w_vo[:, :width]) + bias_v).astype(bf16)
    clips = normed_one.shape[0] // patches
    qk = qk.reshape(clips, patches, -1)
    values = values.reshape(clips, patches, -1)
    if temporal:
        period = patches // lax.axis_size("seq")
        qk = dispatch(qk).reshape(qk.shape)
        values = dispatch(values).reshape(values.shape)
        attended = attend(qk, values, period)
        attended = collect(attended.reshape(clips, -1, period, width))
    else:
        attended = attend(qk, values, None)
    attended = attended.reshape(clips * patches, width)
    w_out = w_vo[:, width:]
    branch = own_total(row_dot(attended, w_out)) + bias_out
    x_mid = x + mods[2] * branch
    normed_two = both_clips(modulate(x_mid, mods[3], mods[4]).astype(bf16))
    pre_a = mm(normed_two, w_up_a) + bias_up[:half]
    pre_b = mm(normed_two, w_up_b) + bias_up[half:]
    hidden_a = jax.nn.gelu(pre_a, approximate=True).astype(bf16)
    hidden_b = jax.nn.gelu(pre_b, approximate=True).astype(bf16)
    mlp = own_total(row_dot(hidden_a, w_down_a) + row_dot(hidden_b, w_down_b)) + bias_down
    x_next = x_mid + mods[5] * mlp
    saved = (
        x, normed_one, qk, values, attended, branch, x_mid, normed_two, pre_a, pre_b,
        hidden_a, hidden_b, mlp, w_out,
    )
    return x_next, saved


def total(rows):
    return jnp.sum(rows, axis=0, dtype=f32)


def layer_backward(g, mods, weights, saved, temporal):
    (w_qk, w_vo), (w_up_a, w_up_b), (w_down_a, w_down_b) = weights
    (
        x, normed_one, qk, values, attended, branch, x_mid, normed_two, pre_a, pre_b,
        hidden_a, hidden_b, mlp, w_out,
    ) = saved
    patches = x.shape[0]
    width = values.shape[-1]
    grad_gate_two = total(g * mlp)
    grad_mlp = both_clips((mods[5] * g).astype(bf16))
    down_grads = [col_dot(grad_mlp, hidden_a).astype(bf16), col_dot(grad_mlp, hidden_b).astype(bf16)]
    pres = []
    for pre, w_down in ((pre_a, w_down_a), (pre_b, w_down_b)):
        back = jax.vjp(partial(jax.nn.gelu, approximate=True), pre)[1]
        pres.append(back(mm(grad_mlp, w_down))[0].astype(bf16))
    up_grads = [col_dot(normed_two, pres[0]).astype(bf16), col_dot(normed_two, pres[1]).astype(bf16)]
    grad_normed_two = own_total(row_dot(pres[0], w_up_a) + row_dot(pres[1], w_up_b))
    back_two = jax.vjp(modulate, x_mid, mods[3], mods[4])[1]
    grad_norm, grad_shift_two, grad_scale_two = back_two(grad_normed_two)
    g_mid = g + grad_norm
    grad_gate_one = total(g_mid * branch)
    grad_branch = both_clips((mods[2] * g_mid).astype(bf16))
    out_grad = col_dot(grad_branch, attended).astype(bf16)
    grad_att = mm(grad_branch, w_out).astype(bf16)
    clips = grad_att.shape[0] // patches
    grad_att = grad_att.reshape(clips, patches, width)
    if temporal:
        period = patches // lax.axis_size("seq")
        grad_att = dispatch(grad_att).reshape(grad_att.shape)
        grad_qk, grad_v = attend_grad(qk, values, grad_att, period)
        pair_grad = jnp.stack([total(grad_qk.reshape(-1, 2 * width)[:, :width]), total(grad_v.reshape(-1, width))])
        grad_qk = collect(grad_qk.reshape(clips, -1, period, 2 * width))
        grad_v = collect(grad_v.reshape(clips, -1, period, width))
    else:
        grad_qk, grad_v = attend_grad(qk, values, grad_att, None)
        pair_grad = jnp.stack([total(grad_qk.reshape(-1, 2 * width)[:, :width]), total(grad_v.reshape(-1, width))])
    grad_qk = grad_qk.reshape(clips * patches, 2 * width)
    grad_v = grad_v.reshape(clips * patches, width)
    qk_grad = col_dot(normed_one, grad_qk).astype(bf16)
    v_grad = col_dot(normed_one, grad_v).astype(bf16)
    grad_normed_one = own_total(row_dot(grad_qk, w_qk) + row_dot(grad_v, w_vo[:, :width]))
    back_one = jax.vjp(modulate, x, mods[0], mods[1])[1]
    grad_norm, grad_shift_one, grad_scale_one = back_one(grad_normed_one)
    g_below = g_mid + grad_norm
    mod_grads = jnp.stack(
        [grad_shift_one, grad_scale_one, grad_gate_one, grad_shift_two, grad_scale_two, grad_gate_two]
    )
    bias_grads = (
        pair_grad,
        total(grad_branch),
        jnp.concatenate([total(pres[0]), total(pres[1])]),
        total(grad_mlp),
    )
    grads = (down_grads, up_grads, [qk_grad, jnp.concatenate([v_grad, out_grad], axis=1)])
    return g_below, mod_grads, bias_grads, grads


def shards(
    tokens,
    conditioning,
    cotangent,
    modulation_weight,
    modulation_bias,
    triple_weight,
    pair_bias,
    out_weight,
    out_bias,
    hidden_weight,
    hidden_bias,
    output_weight,
    output_bias,
):
    layers, _, _, width = triple_weight.shape
    model = tokens.shape[3]
    patches = tokens.shape[2]
    own_clips = tokens.shape[0] // lax.axis_size("tensor")
    all_clips = conditioning.shape[0]
    assert own_clips == 1 and tokens.shape[1] == 1 and layers == 2
    units = hidden_weight.shape[2]
    half = units // 2
    dp_index, seq_index = lax.axis_index("dp"), lax.axis_index("seq")
    core = lax.axis_index("tensor")
    n_dp, n_seq, n_core = lax.axis_size("dp"), lax.axis_size("seq"), lax.axis_size("tensor")

    def unit(layer, which):
        if which == 0:
            triple = triple_weight[layer]
            first = jnp.concatenate([triple[:, 0], triple[:, 1]], axis=1)
            second = jnp.concatenate([triple[:, 2], out_weight[layer].T], axis=1)
        else:
            rows = hidden_weight[layer] if which == 1 else output_weight[layer].T
            first, second = rows[:, :half], rows[:, half:]
        return jnp.stack([first, second])

    shard = [[unit(layer, which) for which in range(3)] for layer in range(layers)]
    gathered = [[None] * 3 for _ in range(layers)]
    dp_order = list(reversed(range(bits_of(n_dp))))
    first_blocks = jnp.stack(gather_tree(shard[0][0], "dp", dp_order), axis=1)
    gathered[0][0] = finish_gather([first_blocks[0], first_blocks[1]], dp_index, seq_index)

    act_cond, silu_back = jax.vjp(jax.nn.silu, conditioning)
    act_low = act_cond.astype(bf16)
    local_term = jnp.einsum("cd,lde->cle", act_low, modulation_weight, preferred_element_type=f32)
    bias_cols = modulation_bias.shape[1]
    offset = ((dp_index * n_seq + seq_index) * n_core + core) * bias_cols
    bias_full = lax.dynamic_update_slice(
        jnp.zeros((layers, local_term.shape[2]), f32), modulation_bias.astype(f32), (jnp.int32(0), offset)
    )
    contribution = (local_term + bias_full[None]).reshape(n_dp, n_core, -1)
    contribution = take(contribution, 1, core) + swap(take(contribution, 1, 1 - core))
    mods = sum_small(scatter_small(contribution, "dp"), "seq").reshape(layers, 6, model)

    packed = jnp.concatenate(
        [pair_bias.reshape(layers, -1), out_bias, hidden_bias.reshape(layers, -1), output_bias], axis=1
    )
    spread = gather_small(gather_small(packed, "seq"), "dp").reshape(n_dp * n_seq, layers, -1)
    cuts, at = [], 0
    for size in (pair_bias.shape[3], pair_bias.shape[3], out_bias.shape[1], hidden_bias.shape[2], output_bias.shape[1]):
        cuts.append(spread[:, :, at : at + size].transpose(1, 0, 2).reshape(layers, -1).astype(f32))
        at += size

    late = [[(0, 1), (0, 2)], [(1, 0), (1, 1), (1, 2)]]
    for group in late:
        stacked = jnp.concatenate([shard[layer][which] for layer, which in group])
        blocks = lax.all_gather(stacked, "dp", axis=1)
        for pos, (layer, which) in enumerate(group):
            gathered[layer][which] = finish_gather([blocks[2 * pos], blocks[2 * pos + 1]], None, seq_index)

    x = take(tokens, 0, core).reshape(patches, model).astype(f32)
    kept = []
    for layer in range(layers):
        biases = [cut[layer] for cut in cuts]
        x, saved = layer_forward(x, mods[layer], gathered[layer], biases, layer == 1)
        kept.append(saved)

    def to_both(own):
        other = swap(own)
        pair = jnp.stack([jnp.where(core == 0, own, other), jnp.where(core == 0, other, own)])
        return pair.reshape((2, 1) + own.shape)

    activations = to_both(x.astype(bf16))
    g = take(cotangent, 0, core).reshape(patches, model).astype(f32)
    mod_grads, bias_grads = [None] * layers, [None] * layers
    done = [[None] * 3 for _ in range(layers)]

    def reduce_units(pairs, tree):
        blocks = [scatter_seq(grad, which) for pair in pairs for which, grad in enumerate(pair)]
        stacked = jnp.stack(blocks, axis=1)
        if tree:
            return scatter_dp_tree(stacked)
        return lax.psum_scatter(stacked, "dp", scatter_dimension=0)

    for layer in reversed(range(layers)):
        g, mod_grads[layer], bias_grads[layer], grads = layer_backward(
            g, mods[layer], gathered[layer], kept[layer], layer == 1
        )
        mlp_units = reduce_units(grads[:2], False)
        done[layer][2] = mlp_units[:2]
        done[layer][1] = mlp_units[2:]
        done[layer][0] = reduce_units(grads[2:], layer == 0)
    input_grad = to_both(g)

    def stack_layers(which, build):
        return jnp.stack([build(done[layer][which].astype(f32)) for layer in range(layers)])

    triple_grad = stack_layers(
        0, lambda u: jnp.stack([u[0][:, :width], u[0][:, width:], u[1][:, :width]], axis=1)
    )
    out_grad = stack_layers(0, lambda u: u[1][:, width:].T)
    hidden_grad = stack_layers(1, lambda u: jnp.concatenate([u[0], u[1]], axis=1))
    output_grad = stack_layers(2, lambda u: jnp.concatenate([u[0], u[1]], axis=1).T)

    def cut_rows(rows):
        return rows.reshape(rows.shape[:-1] + (n_dp * n_seq, -1))

    packed_grads = []
    for layer in range(layers):
        pair_grad, grad_out_bias, grad_up_bias, grad_down_bias = (cut_rows(b) for b in bias_grads[layer])
        packed_grads.append(
            jnp.concatenate([pair_grad[0], pair_grad[1], grad_out_bias, grad_up_bias, grad_down_bias], axis=1)
        )
    bias_rows = jnp.stack(packed_grads, axis=1).reshape(n_dp, n_seq, layers, -1)
    bias_rows = scatter_small(scatter_small(bias_rows.transpose(1, 0, 2, 3), "seq"), "dp")
    sizes = (2 * pair_bias.shape[3], out_bias.shape[1], hidden_bias.shape[2], output_bias.shape[1])
    ends = [sum(sizes[: i + 1]) for i in range(4)]
    pair_out = bias_rows[:, : ends[0]].reshape(layers, 2, 1, -1)
    out_bias_grad = bias_rows[:, ends[0] : ends[1]]
    hidden_bias_grad = bias_rows[:, ends[1] : ends[2]].reshape(layers, 1, -1)
    output_bias_grad = bias_rows[:, ends[2] : ends[3]]

    own_mods = sum_small(jnp.stack(mod_grads).reshape(-1), "seq").astype(bf16)
    grad_mods = gather_small(gather_small(own_mods, "tensor"), "dp").reshape(all_clips, layers, -1)
    modulation_weight_grad = jnp.einsum("cd,cle->lde", act_low, grad_mods, preferred_element_type=f32)
    modulation_bias_grad = lax.dynamic_slice_in_dim(
        jnp.sum(grad_mods, axis=0, dtype=f32), offset, bias_cols, 1
    )
    grad_act = jnp.einsum("cle,lde->cd", grad_mods, modulation_weight, preferred_element_type=f32)
    cond_grad = silu_back(grad_act)[0]
    return (
        activations,
        input_grad,
        cond_grad,
        modulation_weight_grad,
        modulation_bias_grad,
        triple_grad,
        pair_out,
        out_grad,
        out_bias_grad,
        hidden_grad,
        hidden_bias_grad,
        output_grad,
        output_bias_grad,
    )


def solution(mesh):
    owners = ("dp", "seq")
    everyone = ("dp", "seq", "tensor")
    rows = P("dp", "seq", None, None)
    weights = (
        P(None, everyone, None),
        P(None, everyone),
        P(None, owners, None, "tensor"),
        P(None, None, "tensor", owners),
        P(None, "tensor", owners),
        P(None, owners),
        P(None, owners, "tensor"),
        P(None, "tensor", owners),
        P(None, "tensor", owners),
        P(None, owners),
    )
    return jax.shard_map(
        shards,
        mesh=mesh,
        in_specs=(rows, P(None, everyone), rows) + weights,
        out_specs=(rows, rows, P(None, everyone)) + weights,
        check_vma=False,
    )
```

```python
from functools import partial

import jax
import jax.numpy as jnp
from jax import lax
from jax.experimental import pallas as pl
from jax.experimental.pallas import tpu as pltpu
from jax.sharding import PartitionSpec as P

HEAD_DIM = 72
LANES = 128
EPSILON = 1e-06
MIB = 1024 * 1024
f32 = jnp.float32
bf16 = jnp.bfloat16
LIGHT = pl.CostEstimate(flops=1, bytes_accessed=1, transcendentals=0)
GELU_C = 0.7978845608028654


class Flow:
    RATE = 0.0435
    SEND = 1.5

    def __init__(self):
        self.now = 0.0
        self.busy = {}
        self.queues = {}
        self.fresh = []
        self.before = None
        self.latest = []
        self.last = {}
        self.depth = 1
        self.held = False

    def post(self, value, axis, bit, then, rank, weight=1.0):
        line = (axis, bit) if axis == "seq" else (axis, 0)
        size = value.size * value.dtype.itemsize * weight / (self.RATE * 1e6)
        queue = self.queues.setdefault(line, [])
        queue.append((value, axis, bit, size, then, rank))
        queue.sort(key=lambda entry: entry[-1])
        self.begin()

    def begin(self):
        for line, queue in self.queues.items():
            busy = self.busy.setdefault(line, [])
            depth = self.depth if line[0] == "seq" else 1
            while queue and len(busy) < depth and not (self.held and line[0] == "seq"):
                value, axis, bit, duration, then, _ = queue.pop(0)
                ahead = self.last.get(line, []) + (self.latest if axis == "seq" else [])
                if ahead:
                    value = lax.optimization_barrier((value, ahead))[0]
                self.now += self.SEND
                start = max([self.now] + [entry[0] for entry in busy])
                busy.append((start + duration, pxor(value, axis, 1 << bit), then))

    def pump(self):
        while True:
            lines = [line for line, busy in self.busy.items() if busy]
            line = min(lines, key=lambda entry: self.busy[entry][0][0], default=None)
            if line is None or self.busy[line][0][0] > self.now:
                break
            _, got, then = self.busy[line].pop(0)
            self.last[line] = [got]
            self.fresh.append(got)
            then(got)
            self.begin()

    def hold(self, cost):
        self.pump()
        self.held = True
        left = [entry[0] for line, busy in self.busy.items() if line[0] == "seq" for entry in busy]
        self.now = max([self.now] + left) + cost

    def release(self, got):
        self.held = False
        self.latest = [got]
        self.begin()
        self.latest = []

    def until(self, ready):
        self.pump()
        while not ready():
            self.now = max(self.now, min(busy[0][0] for busy in self.busy.values() if busy))
            self.pump()

    def step(self, cost, value):
        self.pump()
        if self.before is not None:
            self.fresh.append(self.before)
            self.before = None
        if self.fresh:
            value = lax.optimization_barrier((value, self.fresh))[0]
            self.fresh = []
        self.now += cost
        return value

    def note(self, *arrays):
        self.fresh.extend(arrays)

    def ran(self, outputs):
        self.before = outputs[0]
        return outputs


def bits_of(size):
    return max(size.bit_length() - 1, 0)


def pxor(value, axis, flip):
    size = lax.axis_size(axis)
    return lax.ppermute(value, axis, [(i, i ^ flip) for i in range(size)])


def swap(value):
    return pxor(value, "tensor", 1)


def take(value, axis, index):
    return lax.dynamic_index_in_dim(value, index, axis, keepdims=False)


def place_kernel(cuts, idx_ref, *refs):
    inner = len(refs) - len(cuts)
    blocks, outs = refs[:inner], refs[inner:]
    for rel, block in enumerate(blocks):
        at = jnp.bitwise_xor(idx_ref[1], rel)
        for (top, rows, left, cols, before, after), out_ref in zip(cuts, outs):
            part = block[0, top : top + rows, left : left + cols]
            sides = [part]
            if before:
                sides.insert(0, jnp.zeros((rows, before), part.dtype))
            if after:
                sides.append(jnp.zeros((rows, after), part.dtype))
            out_ref[0, at] = jnp.concatenate(sides, axis=1) if len(sides) > 1 else part


def place(blocks, outer_index, inner_index, cuts=None):
    outer, rows, cols = blocks[0].shape
    inner = len(blocks)
    cuts = cuts or ((0, rows, 0, cols, 0, 0),)
    start = jnp.int32(0) if outer_index is None else outer_index
    index = jnp.stack([start, inner_index]).astype(jnp.int32)
    sizes = [(cut[1], cut[3] + cut[4] + cut[5]) for cut in cuts]
    return pl.pallas_call(
        partial(place_kernel, cuts),
        grid_spec=pltpu.PrefetchScalarGridSpec(
            num_scalar_prefetch=1,
            grid=(outer,),
            in_specs=[pl.BlockSpec((1, rows, cols), lambda o, idx: (o, 0, 0))] * inner,
            out_specs=[
                pl.BlockSpec((1, inner) + size, lambda o, idx: (jnp.bitwise_xor(idx[0], o), 0, 0, 0))
                for size in sizes
            ],
        ),
        out_shape=[jax.ShapeDtypeStruct((outer, inner) + size, blocks[0].dtype) for size in sizes],
        compiler_params=pltpu.CompilerParams(vmem_limit_bytes=12 * MIB),
        cost_estimate=LIGHT,
        name="place",
    )(index, *blocks)


class Gather:
    def __init__(self, flow, rank, halves, dp_index, seq_index, cuts, cost):
        self.rank = rank
        self.flow, self.index, self.cuts, self.cost = flow, (dp_index, seq_index), cuts, cost
        self.count, self.outer = bits_of(lax.axis_size("seq")), bits_of(lax.axis_size("dp"))
        self.blocks = {}
        self.trees = [{}, {}]
        self.along_dp(0, self.outer, halves)

    def along_dp(self, rel, below, block):
        self.blocks[rel] = block
        for bit in reversed(range(below)):
            self.flow.post(
                block, "dp", bit, partial(self.along_dp, rel | 1 << bit, bit), self.rank, 1.0 + bit
            )
        if len(self.blocks) == 1 << self.outer:
            ordered = [self.blocks[r] for r in range(1 << self.outer)]
            self.flow.now += 2.0
            for which in range(2):
                stacked = jnp.stack([block[which] for block in ordered])
                self.along_seq(which, 0, 0, stacked)

    def along_seq(self, which, rel, first, block):
        self.trees[which][rel] = block
        for step in range(first, self.count):
            bit = step if which == 0 else self.count - 1 - step
            self.flow.post(block, "seq", bit, partial(self.along_seq, which, rel | 1 << bit, step + 1), self.rank)

    def ready(self):
        return all(len(tree) == 1 << self.count for tree in self.trees)

    def result(self):
        self.flow.until(self.ready)
        results = []
        for which in range(2):
            ordered = [self.trees[which][rel] for rel in range(1 << self.count)]
            ordered[0] = self.flow.step(self.cost, ordered[0])
            placed = self.flow.ran(place(ordered, *self.index, self.cuts[which]))
            results.append([p.reshape(-1, p.shape[-1]) for p in placed])
        return results


def add_up(parts):
    return sum(part.astype(f32) for part in parts[1:]) + parts[0].astype(f32)


class Scatter:
    def __init__(self, flow, rank):
        self.flow, self.rank = flow, rank
        self.count, self.outer = bits_of(lax.axis_size("seq")), bits_of(lax.axis_size("dp"))
        self.halves = [None, None]
        self.total = None

    def give(self, which, kept, sent):
        order = list(range(self.count))
        if which == 0:
            order.reverse()
        left = [bit for bit in reversed(range(self.count)) if bit != order[0]]
        shape = kept.shape[:1] + (2,) * (self.count - 1) + kept.shape[2:]
        self.flow.post(
            sent,
            "seq",
            order[0],
            lambda got: self.along_seq(which, order[1:], left, [kept.reshape(shape), got.reshape(shape)]),
            self.rank,
        )

    def split(self, parts, axis, bit, dim):
        mine = (lax.axis_index(axis) >> bit) & 1
        away = add_up([take(part, dim, 1 - mine) for part in parts]).astype(bf16)
        self.flow.note(away)
        kept = add_up([take(part, dim, mine) for part in parts]).astype(bf16)
        return kept, away

    def along_seq(self, which, order, left, parts):
        if not order:
            self.halves[which] = parts
            if all(half is not None for half in self.halves):
                both = [jnp.stack(pair) for pair in zip(*self.halves)]
                both = [v.reshape((2,) + (2,) * self.outer + v.shape[2:]) for v in both]
                self.along_dp(0, both)
            return
        self.flow.now += 2.0
        bit = order[0]
        kept, away = self.split(parts, "seq", bit, 1 + left.index(bit))
        rest = [b for b in left if b != bit]
        self.flow.post(away, "seq", bit, lambda got: self.along_seq(which, order[1:], rest, [kept, got]), self.rank)

    def along_dp(self, bit, parts):
        if bit == self.outer:
            self.total = add_up(parts)
            return
        self.flow.now += 2.0
        kept, away = self.split(parts, "dp", bit, self.outer - bit)
        self.flow.post(away, "dp", bit, lambda got: self.along_dp(bit + 1, [kept, got]), self.rank, 1.0 + bit)


def scatter_small(value, axis):
    count = bits_of(lax.axis_size(axis))
    value = value.reshape((2,) * count + value.shape[1:])
    for bit in reversed(range(count)):
        mine = (lax.axis_index(axis) >> bit) & 1
        value = take(value, 0, mine) + pxor(take(value, 0, 1 - mine), axis, 1 << bit)
    return value


def sum_small(value, axis):
    for bit in range(bits_of(lax.axis_size(axis))):
        value = value + pxor(value, axis, 1 << bit)
    return value


def gather_small(value, axis):
    for bit in range(bits_of(lax.axis_size(axis))):
        value = jnp.concatenate([value, pxor(value, axis, 1 << bit)], axis=0)
    return value


def dispatch(arrays):
    size, index = lax.axis_size("seq"), lax.axis_index("seq")
    parts = []
    for rel in range(size):
        views = [a.reshape(a.shape[0], size, a.shape[1] // size, a.shape[2]) for a in arrays]
        taken = [take(view, 1, index ^ rel) for view in views]
        part = jnp.concatenate(taken, axis=-1) if len(taken) > 1 else taken[0]
        parts.append(part if rel == 0 else pxor(part, "seq", rel))
    stacked = jnp.stack(parts, axis=1)
    return stacked.reshape(stacked.shape[0], -1, stacked.shape[-1])


def collect(rows, cuts):
    size, index = lax.axis_size("seq"), lax.axis_index("seq")
    parts = rows.reshape(rows.shape[0], size, rows.shape[1] // size, rows.shape[2])
    blocks = []
    for rel in range(size):
        block = parts[:, rel]
        blocks.append(block if rel == 0 else pxor(block, "seq", rel))
    return [p.reshape(-1, p.shape[-1]) for p in place(blocks, None, index, cuts)]


def head_windows(width):
    spans = []
    for first in range(0, width, HEAD_DIM):
        low = first // LANES * LANES
        high = min(-(-(first + HEAD_DIM) // LANES) * LANES, width)
        spans.append((first, low, high))
    return spans


def head_mask(first, low, high):
    lane = lax.broadcasted_iota(jnp.int32, (1, high - low), 1) + low
    return jnp.where((lane >= first) & (lane < first + HEAD_DIM), 1.0, 0.0).astype(bf16)


def row_dot(left, right):
    return lax.dot_general(left, right, (((1,), (1,)), ((), ())), preferred_element_type=f32)


def col_dot(left, right):
    return lax.dot_general(left, right, (((0,), (0,)), ((), ())), preferred_element_type=f32)


def softmax_probs(queries, key_rows, apart):
    scores = row_dot(queries, key_rows) * (HEAD_DIM ** (-0.5))
    if apart is not None:
        scores = jnp.where(apart, -1e30, scores)
    top = jnp.max(scores, axis=-1, keepdims=True)
    weights = jnp.exp(scores - top)
    return weights * (1.0 / jnp.sum(weights, axis=-1, keepdims=True))


def tokens_apart(rows, period):
    if period is None:
        return None
    one = lax.broadcasted_iota(jnp.int32, (rows, rows), 0)
    two = lax.broadcasted_iota(jnp.int32, (rows, rows), 1)
    return lax.rem(one, period) != lax.rem(two, period)


def attend_kernel(period, lead, qk_ref, v_ref, out_ref, acc_ref):
    rows, width = acc_ref.shape
    apart = tokens_apart(rows, period)
    queries, key_rows = qk_ref[0, :, :width], qk_ref[0, :, width : 2 * width]
    value_rows = v_ref[0, :, lead : lead + width]
    acc_ref[...] = jnp.zeros_like(acc_ref)
    for first, low, high in head_windows(width):
        mask = head_mask(first, low, high)
        probs = softmax_probs(queries[:, low:high] * mask, key_rows[:, low:high], apart)
        acc_ref[:, low:high] += jnp.dot(
            probs.astype(bf16), value_rows[:, low:high] * mask, preferred_element_type=f32
        )
    attended = acc_ref[...].astype(bf16)
    before = out_ref.shape[2] - width
    if before:
        attended = jnp.concatenate([jnp.zeros((rows, before), bf16), attended], axis=1)
    out_ref[0] = attended


def attend(qk, values, lead, width, before, period):
    blocks, rows = qk.shape[:2]

    def whole(cols):
        return pl.BlockSpec((1, rows, cols), lambda b: (b, 0, 0))

    return pl.pallas_call(
        partial(attend_kernel, period, lead),
        grid=(blocks,),
        out_shape=jax.ShapeDtypeStruct((blocks, rows, before + width), bf16),
        in_specs=[whole(qk.shape[2]), whole(values.shape[2])],
        out_specs=whole(before + width),
        scratch_shapes=[pltpu.VMEM((rows, width), f32)],
        compiler_params=pltpu.CompilerParams(vmem_limit_bytes=24 * MIB),
        cost_estimate=LIGHT,
        name="attend",
    )(qk, values)


def attend_grad_kernel(period, lead, skip, qk_ref, v_ref, da_ref, *refs):
    outs, sum_ref, (acc_q, acc_k, acc_v) = refs[:-4], refs[-4], refs[-3:]
    rows, width = acc_q.shape
    apart = tokens_apart(rows, period)
    queries, key_rows = qk_ref[0, :, :width], qk_ref[0, :, width : 2 * width]
    value_rows = v_ref[0, :, lead : lead + width]
    grad_att = da_ref[0, :, skip : skip + width]
    factor = HEAD_DIM ** (-0.5)
    for acc in (acc_q, acc_k, acc_v):
        acc[...] = jnp.zeros_like(acc)
    for first, low, high in head_windows(width):
        mask = head_mask(first, low, high)
        q_own = queries[:, low:high] * mask
        k_own = key_rows[:, low:high] * mask
        g_own = grad_att[:, low:high] * mask
        probs = softmax_probs(q_own, k_own, apart)
        grad_probs = row_dot(g_own, value_rows[:, low:high])
        inner = jnp.sum(grad_probs * probs, axis=-1, keepdims=True)
        grad_scores = (probs * (grad_probs - inner)).astype(bf16)
        acc_q[:, low:high] += jnp.dot(grad_scores, k_own, preferred_element_type=f32)
        acc_k[:, low:high] += col_dot(grad_scores, q_own)
        acc_v[:, low:high] += col_dot(probs.astype(bf16), g_own)
    grad_q = (acc_q[...] * factor).astype(bf16)
    outs[0][0, :, :width] = grad_q
    outs[0][0, :, width : 2 * width] = (acc_k[...] * factor).astype(bf16)
    grad_v = acc_v[...].astype(bf16)
    if len(outs) == 1:
        outs[0][0, :, 2 * width :] = grad_v
    else:
        outs[1][0] = jnp.concatenate([grad_v, jnp.zeros_like(grad_v)], axis=1)
    sum_ref[0, 0:1, :] = jnp.sum(grad_q.astype(f32), axis=0, keepdims=True)
    sum_ref[0, 1:2, :] = jnp.sum(grad_v.astype(f32), axis=0, keepdims=True)


def attend_grad(qk, values, lead, grad_att, skip, width, period):
    blocks, rows = qk.shape[:2]

    def whole(cols):
        return pl.BlockSpec((1, rows, cols), lambda b: (b, 0, 0))

    cols = [3 * width] if period else [2 * width, 2 * width]
    return pl.pallas_call(
        partial(attend_grad_kernel, period, lead, skip),
        grid=(blocks,),
        out_shape=[jax.ShapeDtypeStruct((blocks, rows, c), bf16) for c in cols]
        + [jax.ShapeDtypeStruct((blocks, 2, width), f32)],
        in_specs=[whole(qk.shape[2]), whole(values.shape[2]), whole(grad_att.shape[2])],
        out_specs=[whole(c) for c in cols] + [pl.BlockSpec((1, 2, width), lambda b: (b, 0, 0))],
        scratch_shapes=[pltpu.VMEM((rows, width), f32)] * 3,
        compiler_params=pltpu.CompilerParams(vmem_limit_bytes=24 * MIB),
        cost_estimate=LIGHT,
        name="attend_grad",
    )(qk, values, grad_att)


def on_chip():
    return pl.BlockSpec(memory_space=pltpu.VMEM)


def in_place():
    return pl.BlockSpec(memory_space=pl.ANY)


def call(kernel, name, inputs, streamed, outs, scratch=(), limit=24, out_specs=None):
    buffers = [pltpu.VMEM(w.shape, w.dtype) for w in streamed]
    sems = [pltpu.SemaphoreType.DMA((len(streamed),))] if streamed else []
    n_in, n_w, n_out = len(inputs), len(streamed), len(outs)

    def body(*refs):
        ins, away = refs[:n_in], refs[n_in : n_in + n_w]
        results = refs[n_in + n_w : n_in + n_w + n_out]
        rest = refs[n_in + n_w + n_out :]
        here, rest = rest[:n_w], rest[n_w:]
        copies = []
        if n_w:
            sem, rest = rest[0], rest[1:]
            copies = [pltpu.make_async_copy(a, h, sem.at[i]) for i, (a, h) in enumerate(zip(away, here))]
            for copy in copies:
                copy.start()

        def fetch(i):
            copies[i].wait()
            return here[i]

        kernel(ins, fetch, results, rest)

    return pl.pallas_call(
        body,
        out_shape=[jax.ShapeDtypeStruct(shape, dtype) for shape, dtype in outs],
        in_specs=[on_chip()] * n_in + [in_place()] * n_w,
        out_specs=out_specs or [on_chip()] * n_out,
        scratch_shapes=buffers + sems + list(scratch),
        compiler_params=pltpu.CompilerParams(vmem_limit_bytes=limit * MIB),
        cost_estimate=LIGHT,
        name=name,
    )(*inputs, *streamed)


def norm_parts(values):
    average = jnp.mean(values, axis=-1, keepdims=True)
    centered = values - average
    variance = jnp.mean(centered * centered, axis=-1, keepdims=True)
    inverse = lax.rsqrt(variance + EPSILON)
    return centered * inverse, inverse


def both(one, two):
    return jnp.concatenate([one[...], two[...]], axis=0)


def modulated(values, mods_ref, shift, scale):
    normed, _ = norm_parts(values)
    return (normed * (1.0 + mods_ref[scale : scale + 1, :]) + mods_ref[shift : shift + 1, :]).astype(bf16)


def norm_forward(x, mods, shift, scale):
    def kernel(ins, fetch, outs, scratch):
        outs[0][...] = modulated(ins[0][...], ins[1], shift, scale)

    return call(kernel, "norm_forward", [x, mods], [], [(x.shape, bf16)])[0]


def project_heads(normed, w_qk, w_vo, biases, row):
    rows, cols = 2 * normed[0].shape[0], w_qk.shape[1]

    def kernel(ins, fetch, outs, scratch):
        tokens = both(ins[0], ins[1])
        for i in range(2):
            bias = ins[2][row + i : row + i + 1, :]
            outs[i][...] = (jnp.dot(tokens, fetch(i)[...], preferred_element_type=f32) + bias).astype(bf16)

    return call(kernel, "project_heads", [*normed, biases], [w_qk, w_vo], [((rows, cols), bf16)] * 2)


def project_back(pairs, dtype, name):
    rows, cols = pairs[0][0].shape[0] // 2, pairs[0][1].shape[0]
    count = len(pairs)

    def kernel(ins, fetch, outs, scratch):
        out = row_dot(ins[0][...], fetch(0)[...])
        for i in range(1, count):
            out = out + row_dot(ins[i][...], fetch(i)[...])
        outs[0][...] = out[:rows]
        outs[1][...] = out[rows:].astype(dtype)

    return call(
        kernel, name, [p[0] for p in pairs], [p[1] for p in pairs], [((rows, cols), f32), ((rows, cols), dtype)]
    )


def residual(x, own, other, biases, bias_row, mods, gate, following):
    def kernel(ins, fetch, outs, scratch):
        branch = ins[1][...] + ins[2][...].astype(f32) + ins[3][bias_row : bias_row + 1, :]
        value = ins[0][...] + ins[4][gate : gate + 1, :] * branch
        outs[0][...] = branch
        outs[1][...] = value
        if following is None:
            outs[2][...] = value.astype(bf16)
        else:
            outs[2][...] = modulated(value, ins[4], *following)

    return call(
        kernel, "residual", [x, own, other, biases, mods], [], [(x.shape, f32), (x.shape, f32), (x.shape, bf16)]
    )


def gelu_parts(pre):
    inner = jnp.tanh(GELU_C * (pre + 0.044715 * (pre * pre * pre)))
    return inner


def mlp_forward(normed, up_a, up_b, down_a, down_b, biases, row, dtype):
    patches, cols = normed[0].shape[0], up_a.shape[1]
    model = down_a.shape[0]
    rows = 2 * patches

    def kernel(ins, fetch, outs, scratch):
        tokens = both(ins[0], ins[1])
        out = None
        for i in range(2):
            bias = ins[2][row + i : row + i + 1, :]
            pre = jnp.dot(tokens, fetch(2 * i)[...], preferred_element_type=f32) + bias
            outs[i][...] = pre
            hidden = (0.5 * pre * (1.0 + gelu_parts(pre))).astype(bf16)
            outs[2 + i][...] = hidden
            part = row_dot(hidden, fetch(2 * i + 1)[...])
            out = part if out is None else out + part
        outs[4][...] = out[:patches]
        outs[5][...] = out[patches:].astype(dtype)

    return call(
        kernel,
        "mlp_forward",
        [*normed, biases],
        [up_a, down_a, up_b, down_b],
        [((rows, cols), f32)] * 2 + [((rows, cols), bf16)] * 2 + [((patches, model), f32), ((patches, model), dtype)],
        limit=48,
    )


def mlp_backward(grad, pre, up, down, so_far):
    patches, model = grad[0].shape
    rows, cols = pre.shape
    last = so_far is not None

    def kernel(ins, fetch, outs, scratch):
        tokens = both(ins[0], ins[1])
        grad_hidden = jnp.dot(tokens, fetch(0)[...], preferred_element_type=f32)
        value = fetch(1)[...]
        inner = gelu_parts(value)
        slope = 0.5 * (1.0 + inner) + 0.5 * value * (1.0 - inner * inner) * (
            GELU_C * (1.0 + 3.0 * 0.044715 * (value * value))
        )
        grad_pre = (grad_hidden * slope).astype(bf16)
        outs[0][...] = grad_pre
        outs[1][0:1, :] = jnp.sum(grad_pre.astype(f32), axis=0, keepdims=True)
        outs[1][1:2, :] = jnp.sum(tokens.astype(f32), axis=0, keepdims=True)
        out = row_dot(grad_pre, fetch(2)[...])
        if last:
            out = out + fetch(3)[...]
            outs[2][...] = out[:patches]
            outs[3][...] = out[patches:].astype(bf16)
        else:
            outs[2][...] = out

    tail = [((patches, model), f32), ((patches, model), bf16)] if last else [((rows, model), f32)]
    return call(
        kernel,
        "mlp_backward",
        list(grad),
        [down, pre, up] + ([so_far] if last else []),
        [((rows, cols), bf16), ((2, cols), f32)] + tail,
        limit=32,
    )


def grad_heads(grad, w_vo):
    patches, model = grad[0].shape
    cols = w_vo.shape[1]

    def kernel(ins, fetch, outs, scratch):
        tokens = both(ins[0], ins[1])
        outs[1][...] = jnp.sum(tokens.astype(f32), axis=0, keepdims=True)
        outs[0][...] = jnp.dot(tokens, fetch(0)[...], preferred_element_type=f32).astype(bf16)

    return call(kernel, "grad_heads", list(grad), [w_vo], [((2 * patches, cols), bf16), ((1, model), f32)])


def norm_backward(g, own, other, x, mods, scale, gate, branch):
    rows, model = x.shape

    def kernel(ins, fetch, outs, scratch):
        grad = ins[1][...] + ins[2][...].astype(f32)
        normed, inverse = norm_parts(ins[3][...])
        scaled = grad * (1.0 + ins[4][scale : scale + 1, :])
        mean_one = jnp.mean(scaled, axis=-1, keepdims=True)
        mean_two = jnp.mean(scaled * normed, axis=-1, keepdims=True)
        value = ins[0][...] + inverse * (scaled - mean_one - normed * mean_two)
        outs[0][...] = value
        outs[1][0:1, :] = jnp.sum(grad, axis=0, keepdims=True)
        outs[1][1:2, :] = jnp.sum(grad * normed, axis=0, keepdims=True)
        if gate is not None:
            outs[1][2:3, :] = jnp.sum(value * ins[5][...], axis=0, keepdims=True)
            outs[2][...] = (ins[4][gate : gate + 1, :] * value).astype(bf16)

    inputs = [g, own, other, x, mods] + ([] if gate is None else [branch])
    outs = [(x.shape, f32), ((3, model), f32)] + ([] if gate is None else [(x.shape, bf16)])
    return call(kernel, "norm_backward", inputs, [], outs)


def insert_bit(rest, bit):
    low = rest & ((1 << bit) - 1)
    return (rest - low) * 2 + low


def weight_grad(pairs, bit, name):
    clusters, parts = lax.axis_size("dp"), lax.axis_size("seq")
    model, cols = pairs[0][0].shape[1], pairs[0][1].shape[1]
    rows = model // (clusters * parts)
    mine = ((lax.axis_index("seq") >> bit) & 1).astype(jnp.int32).reshape(1)
    shape = (clusters, parts // 2, rows, cols)
    count = len(pairs)

    def body(mine_ref, *refs):
        ins, outs, (whole, sem) = refs[: 2 * count], refs[2 * count : 2 * count + 2], refs[2 * count + 2 :]
        out = col_dot(ins[0][...], ins[1][...])
        for i in range(1, count):
            out = out + col_dot(ins[2 * i][...], ins[2 * i + 1][...])
        copies = []
        for c in range(clusters):
            for part in range(parts):
                at = (c * parts + part) * rows
                whole[c * parts + part] = out[at : at + rows].astype(bf16)
        for c in range(clusters):
            for rest in range(parts // 2):
                start = c * parts + insert_bit(rest, bit)
                for which in range(2):
                    side = mine_ref[0] if which == 0 else 1 - mine_ref[0]
                    copy = pltpu.make_async_copy(
                        whole.at[start + (side << bit)],
                        outs[which].at[c, rest],
                        sem.at[(c * (parts // 2) + rest) * 2 + which],
                    )
                    copy.start()
                    copies.append(copy)
        for copy in copies:
            copy.wait()

    return pl.pallas_call(
        body,
        out_shape=[jax.ShapeDtypeStruct(shape, bf16)] * 2,
        in_specs=[pl.BlockSpec(memory_space=pltpu.SMEM)] + [on_chip()] * (2 * count),
        out_specs=[in_place()] * 2,
        scratch_shapes=[
            pltpu.VMEM((clusters * parts, rows, cols), bf16),
            pltpu.SemaphoreType.DMA((clusters * parts,)),
        ],
        compiler_params=pltpu.CompilerParams(vmem_limit_bytes=32 * MIB),
        cost_estimate=LIGHT,
        name=name,
    )(mine, *[array for pair in pairs for array in pair])


def with_other(flow, own):
    flow.now += 5.0
    return own, swap(own)


def dispatch_in(flow, arrays, cost, hold):
    arrays[0] = flow.step(2.0, arrays[0])
    if hold:
        flow.hold(cost)
        result = dispatch(arrays)
        flow.release(result)
        return result
    flow.now += 2.5 * cost
    return dispatch(arrays)


def collect_in(flow, rows, cuts, cost, hold):
    rows = flow.step(2.0, rows)
    if hold:
        flow.hold(cost)
        result = collect(rows, cuts)
        flow.release(result[0])
        return result
    flow.now += 2.5 * cost
    return collect(rows, cuts)


def layer_forward(flow, x, normed_one, mods, layer, units, biases_of, temporal, following):
    attention_unit, mlp_unit = units
    patches = x.shape[0]
    base = 6 * layer
    normed_one = with_other(flow, normed_one)
    w_qk, w_vo = attention_unit()
    width = w_qk.shape[1] // 2
    biases = biases_of()
    qk, vo = flow.ran(project_heads((flow.step(6.5, normed_one[0]), normed_one[1]), w_qk, w_vo, biases, base))
    qk = qk.reshape(2, patches, -1)
    vo = vo.reshape(2, patches, -1)
    if temporal:
        period = patches // lax.axis_size("seq")
        qkv = dispatch_in(flow, [qk, vo[:, :, :width]], 17.0, False)
        heads = (flow.step(3.5, qkv), qkv, 2 * width)
        attended = attend(*heads, width, 0, period)
        attended = collect_in(flow, attended, ((0, period, 0, width, width, 0),), 11.0, False)[0]
    else:
        heads = (flow.step(3.5, qk), vo, 0)
        attended = attend(*heads, width, width, None).reshape(2 * patches, -1)
    own, other = flow.ran(project_back([(flow.step(2.5, attended), w_vo)], f32, "project_out"))
    other = swap(other)
    flow.now += 5.0
    branch, x_mid, normed_two = flow.ran(
        residual(x, flow.step(2.0, own), other, biases, base + 2, mods, base + 2, (base + 3, base + 4))
    )
    normed_two = with_other(flow, normed_two)
    w_up_a, w_up_b, w_down_a, w_down_b = mlp_unit()
    tokens = (flow.step(11.0, normed_two[0]), normed_two[1])
    pre_a, pre_b, hidden_a, hidden_b, own, other = flow.ran(
        mlp_forward(tokens, w_up_a, w_up_b, w_down_a, w_down_b, biases, base + 3, f32)
    )
    other = swap(other)
    flow.now += 5.0
    mlp, x_next, after = flow.ran(
        residual(x_mid, flow.step(2.0, own), other, biases, base + 5, mods, base + 5, following)
    )
    saved = (x, normed_one, heads, attended, branch, x_mid, normed_two, pre_a, pre_b, hidden_a, hidden_b, mlp)
    weights = (w_qk, w_vo, w_up_a, w_up_b, w_down_a, w_down_b)
    return x_next, after, saved, weights


def layer_backward(flow, g, grad_mlp, mods, layer, weights, saved, temporal, below):
    w_qk, w_vo, w_up_a, w_up_b, w_down_a, w_down_b = weights
    x, normed_one, heads, attended, branch, x_mid, normed_two, pre_a, pre_b, hidden_a, hidden_b, _ = saved
    patches = x.shape[0]
    width = w_qk.shape[1] // 2
    base = 6 * layer
    done = [Scatter(flow, 10 - 4 * layer - unit) for unit in range(3)]
    bits = (bits_of(lax.axis_size("seq")) - 1, 0)

    def reduce_half(unit, which, pairs, name):
        first = flow.step(5.0, pairs[0][1])
        done[unit].give(which, *flow.ran(weight_grad([(pairs[0][0], first)] + pairs[1:], bits[which], name)))

    def joined(pair):
        return jnp.concatenate(pair, axis=0)

    grad_mlp = with_other(flow, grad_mlp)
    grad_mlp_rows = joined(grad_mlp)
    reduce_half(2, 0, [(grad_mlp_rows, hidden_a)], "down_grad")
    reduce_half(2, 1, [(grad_mlp_rows, hidden_b)], "down_grad")
    normed_rows = joined(normed_two)
    tokens = (flow.step(7.0, grad_mlp[0]), grad_mlp[1])
    grad_pre_a, sums_a, so_far = flow.ran(mlp_backward(tokens, pre_a, w_up_a, w_down_a, None))
    reduce_half(1, 0, [(normed_rows, grad_pre_a)], "up_grad")
    tokens = (flow.step(8.0, grad_mlp[0]), grad_mlp[1])
    grad_pre_b, sums_b, own, other = flow.ran(mlp_backward(tokens, pre_b, w_up_b, w_down_b, so_far))
    other = swap(other)
    reduce_half(1, 1, [(normed_rows, grad_pre_b)], "up_grad")
    g_mid, sums_two, grad_branch = flow.ran(
        norm_backward(g, flow.step(2.0, own), other, x_mid, mods, base + 4, base + 2, branch)
    )
    other_branch = swap(grad_branch)
    flow.now += 4.0
    grad_branch = (flow.step(2.5, grad_branch), other_branch)
    grad_att, sum_branch = flow.ran(grad_heads(grad_branch, w_vo))
    grad_att = grad_att.reshape(2, patches, -1)
    if temporal:
        period = patches // lax.axis_size("seq")
        grad_att = dispatch_in(flow, [grad_att[:, :, width:]], 10.0, True)
        grad_qkv, sums_pair = flow.ran(attend_grad(*heads, flow.step(10.5, grad_att), 0, width, period))
        cuts = ((0, period, 0, 2 * width, 0, 0), (0, period, 2 * width, width, 0, width))
        grad_qk, grad_v = collect_in(flow, grad_qkv, cuts, 18.0, True)
    else:
        grad_qk, grad_v, sums_pair = flow.ran(
            attend_grad(*heads, flow.step(10.5, grad_att), width, width, None)
        )
        grad_qk = grad_qk.reshape(2 * patches, -1)
        grad_v = grad_v.reshape(2 * patches, -1)
    own, other = flow.ran(
        project_back([(flow.step(5.0, grad_qk), w_qk), (grad_v, w_vo)], bf16, "grad_normed")
    )
    other = swap(other)
    rows_one = joined(normed_one)
    reduce_half(0, 0, [(rows_one, grad_qk)], "heads_grad")
    own = flow.step(2.0, own)
    if below is None:
        g_below, sums_one = flow.ran(norm_backward(g_mid, own, other, x, mods, base + 1, None, None))
        grad_below = None
    else:
        g_below, sums_one, grad_below = flow.ran(
            norm_backward(g_mid, own, other, x, mods, base + 1, base - 1, below)
        )
    reduce_half(0, 1, [(rows_one, grad_v), (joined(grad_branch), attended)], "heads_grad")
    mod_sums = [sums_one[0], sums_one[1], sums_two[2], sums_two[0], sums_two[1]]
    bias_sums = [
        jnp.sum(sums_pair, axis=0).reshape(-1),
        sum_branch.reshape(-1),
        sums_a[0],
        sums_b[0],
        sums_a[1],
    ]
    return g_below, grad_below, mod_sums, sums_one[2], bias_sums, done


def shards(
    tokens,
    conditioning,
    cotangent,
    modulation_weight,
    modulation_bias,
    triple_weight,
    pair_bias,
    out_weight,
    out_bias,
    hidden_weight,
    hidden_bias,
    output_weight,
    output_bias,
):
    layers, _, _, width = triple_weight.shape
    model = tokens.shape[3]
    patches = tokens.shape[2]
    own_clips = tokens.shape[0] // lax.axis_size("tensor")
    all_clips = conditioning.shape[0]
    assert own_clips == 1 and tokens.shape[1] == 1 and layers == 2
    assert model == 2 * width and hidden_weight.shape[2] == 2 * model
    units = hidden_weight.shape[2]
    half = units // 2
    dp_index, seq_index = lax.axis_index("dp"), lax.axis_index("seq")
    core = lax.axis_index("tensor")
    n_dp, n_seq, n_core = lax.axis_size("dp"), lax.axis_size("seq"), lax.axis_size("tensor")

    packed = jnp.concatenate(
        [pair_bias.reshape(layers, -1), out_bias, hidden_bias.reshape(layers, -1), output_bias], axis=1
    ).reshape(-1)
    rows = triple_weight.shape[1]

    def attention_unit(layer):
        triple = triple_weight[layer]
        first = jnp.concatenate([triple[:, 0], triple[:, 1]], axis=1)
        second = jnp.concatenate([triple[:, 2], out_weight[layer].T], axis=1)
        if layer == 0:
            extra = jnp.zeros((8 * 2 * width,), bf16).at[: packed.shape[0]].set(packed).reshape(8, -1)
            first = jnp.concatenate([first, extra])
            second = jnp.concatenate([second, jnp.zeros_like(extra)])
        return jnp.stack([first, second])

    def mlp_unit(layer):
        down = output_weight[layer].T
        up = hidden_weight[layer]
        return jnp.stack(
            [jnp.concatenate([up[:, part], down[:, part]], axis=1) for part in (slice(0, half), slice(half, None))]
        )

    flow = Flow()
    flow.now = 8.0
    gathers = []
    for layer in range(layers):
        whole = (0, rows, 0, 2 * width, 0, 0)
        first_cuts = (whole, (rows, 8, 0, 2 * width, 0, 0)) if layer == 0 else (whole,)
        attention = Gather(flow, 2 * layer, attention_unit(layer), dp_index, seq_index, (first_cuts, (whole,)), 2.0)
        pair_cuts = ((0, rows, 0, half, 0, 0), (0, rows, half, half, 0, 0))
        mlp = Gather(flow, 2 * layer + 1, mlp_unit(layer), dp_index, seq_index, (pair_cuts, pair_cuts), 3.5)
        gathers.append((attention, mlp))

    act_cond, silu_back = jax.vjp(jax.nn.silu, conditioning)
    act_low = act_cond.astype(bf16)
    local_term = jnp.einsum("cd,lde->cle", act_low, modulation_weight, preferred_element_type=f32)
    bias_cols = modulation_bias.shape[1]
    offset = ((dp_index * n_seq + seq_index) * n_core + core) * bias_cols
    bias_full = lax.dynamic_update_slice(
        jnp.zeros((layers, local_term.shape[2]), f32), modulation_bias.astype(f32), (jnp.int32(0), offset)
    )
    contribution = (local_term + bias_full[None]).reshape(n_dp, n_core, -1)
    contribution = take(contribution, 1, core) + swap(take(contribution, 1, 1 - core))
    contribution = flow.step(25.0, contribution)
    mods = sum_small(scatter_small(contribution, "dp"), "seq").reshape(layers * 6, model)

    def unpack(spread):
        spread = spread.reshape(n_dp * n_seq, -1)[:, : packed.shape[0]].reshape(n_dp * n_seq, layers, -1)
        spread = spread.transpose(1, 0, 2).astype(f32)
        cuts, at = [], 0
        for size in (pair_bias.shape[3], pair_bias.shape[3], out_bias.shape[1], hidden_bias.shape[2], output_bias.shape[1]):
            cuts.append(spread[:, :, at : at + size].reshape(layers, -1))
            at += size
        blank = jnp.zeros_like(cuts[0])
        return jnp.concatenate([cuts[0], blank, cuts[1], blank, *cuts[2:]], axis=1).reshape(6 * layers, model)

    found = {}

    def attention_weights(layer):
        first, second = gathers[layer][0].result()
        if layer == 0:
            found["biases"] = unpack(first[1])
        return first[0], second[0]

    def mlp_weights(layer):
        first, second = gathers[layer][1].result()
        return first[0], second[0], first[1], second[1]

    x = take(tokens, 0, core).reshape(patches, model).astype(f32)
    after = norm_forward(x, mods, 0, 1)
    kept, weights = [], []
    for layer in range(layers):
        following = (6 * layer + 6, 6 * layer + 7) if layer + 1 < layers else None
        pending = (partial(attention_weights, layer), partial(mlp_weights, layer))
        x, after, saved, layer_weights = layer_forward(
            flow, x, after, mods, layer, pending, lambda: found["biases"], layer == 1, following
        )
        kept.append(saved)
        weights.append(layer_weights)

    def to_both(own):
        other = swap(own)
        pair = jnp.stack([jnp.where(core == 0, own, other), jnp.where(core == 0, other, own)])
        return pair.reshape((2, 1) + own.shape)

    activations = to_both(after)
    g = take(cotangent, 0, core).reshape(patches, model).astype(f32)
    grad_mlp = (mods[6 * layers - 1] * g).astype(bf16)
    grad_gates = [None] * layers
    grad_gates[-1] = jnp.sum(g * kept[-1][-1], axis=0)
    mod_grads, bias_grads, done = [None] * layers, [None] * layers, [None] * layers
    flow.depth = 2
    for layer in reversed(range(layers)):
        below = kept[layer - 1][-1] if layer else None
        g, grad_mlp, mod_sums, grad_gate, bias_grads[layer], done[layer] = layer_backward(
            flow, g, grad_mlp, mods, layer, weights[layer], kept[layer], layer == 1, below
        )
        mod_grads[layer] = jnp.concatenate(mod_sums + [grad_gates[layer]])
        if layer:
            grad_gates[layer - 1] = grad_gate
    input_grad = to_both(g)
    flow.until(lambda: all(unit.total is not None for layer in range(layers) for unit in done[layer]))

    def stack_layers(which, build):
        return jnp.stack([build(done[layer][which].total) for layer in range(layers)])

    triple_grad = stack_layers(
        0, lambda u: jnp.stack([u[0][:, :width], u[0][:, width:], u[1][:, :width]], axis=1)
    )
    out_grad = stack_layers(0, lambda u: u[1][:, width:].T)
    hidden_grad = stack_layers(1, lambda u: jnp.concatenate([u[0], u[1]], axis=1))
    output_grad = stack_layers(2, lambda u: jnp.concatenate([u[0], u[1]], axis=1).T)

    flat = [part for layer in range(layers) for part in bias_grads[layer]]
    summed = sum_small(jnp.concatenate(mod_grads + flat), "seq").astype(bf16)
    mods_size = 6 * model * layers
    pair = jnp.concatenate([summed[:mods_size], swap(summed[:mods_size]), summed[mods_size:]])
    spread = gather_small(pair.reshape(1, -1, 128), "dp").reshape(n_dp, -1)
    spread = [spread[rel] for rel in range(n_dp)]
    grad_mods = jnp.stack([s[c * mods_size : (c + 1) * mods_size] for s in spread for c in range(n_core)])
    grad_mods = grad_mods.reshape(all_clips, layers, -1)
    clip = jnp.arange(all_clips)
    clip = (clip // n_core ^ dp_index) * n_core + (clip % n_core ^ core)
    bias_sums = add_up([s[n_core * mods_size :] for s in spread]).reshape(layers, -1)
    owner = dp_index * n_seq + seq_index
    bias_out, at = [], 0
    for size, shape in (
        (width, None),
        (width, None),
        (model, out_bias.shape),
        (units, hidden_bias.shape),
        (model, output_bias.shape),
    ):
        part = bias_sums[:, at : at + size].reshape(layers, n_dp * n_seq, -1)
        part = take(part, 1, owner)
        bias_out.append(part if shape is None else part.reshape(shape))
        at += size
    pair_out = jnp.stack(bias_out[:2], axis=1).reshape(pair_bias.shape)
    out_bias_grad, hidden_bias_grad, output_bias_grad = bias_out[2:]
    modulation_weight_grad = jnp.einsum("cd,cle->lde", act_low[clip], grad_mods, preferred_element_type=f32)
    modulation_bias_grad = lax.dynamic_slice_in_dim(
        jnp.sum(grad_mods, axis=0, dtype=f32), offset, bias_cols, 1
    )
    grad_act = jnp.einsum("cle,lde->cd", grad_mods, modulation_weight, preferred_element_type=f32)
    cond_grad = silu_back(grad_act[clip])[0]
    return (
        activations,
        input_grad,
        cond_grad,
        modulation_weight_grad,
        modulation_bias_grad,
        triple_grad,
        pair_out,
        out_grad,
        out_bias_grad,
        hidden_grad,
        hidden_bias_grad,
        output_grad,
        output_bias_grad,
    )


def solution(mesh):
    owners = ("dp", "seq")
    everyone = ("dp", "seq", "tensor")
    rows = P("dp", "seq", None, None)
    weights = (
        P(None, everyone, None),
        P(None, everyone),
        P(None, owners, None, "tensor"),
        P(None, None, "tensor", owners),
        P(None, "tensor", owners),
        P(None, owners),
        P(None, owners, "tensor"),
        P(None, "tensor", owners),
        P(None, "tensor", owners),
        P(None, owners),
    )
    return jax.shard_map(
        shards,
        mesh=mesh,
        in_specs=(rows, P(None, everyone), rows) + weights,
        out_specs=(rows, rows, P(None, everyone)) + weights,
        check_vma=False,
    )
```

```python
from functools import partial

import jax
import jax.numpy as jnp
from jax import lax
from jax.experimental import pallas as pl
from jax.experimental.pallas import tpu as pltpu
from jax.sharding import PartitionSpec as P

HEAD_DIM = 72
LANES = 128
EPSILON = 1e-06
MIB = 1024 * 1024
SCALE = 1.07
SCALE_B = 1.11
TRIP = 1.41
ADD = 4.0
SWAP = 6.0
RATE = 0.0398
SEND = 0.5
DEPTH = 2
HOLD = True
HALF = 0.0
f32 = jnp.float32
bf16 = jnp.bfloat16
LIGHT = pl.CostEstimate(flops=1, bytes_accessed=1, transcendentals=0)
GELU_C = 0.7978845608028654


class Flow:
    def __init__(self):
        self.now = 0.0
        self.busy = {}
        self.queues = {}
        self.fresh = []
        self.before = None
        self.latest = []
        self.last = {}
        self.depth = 1
        self.scale = SCALE
        self.held = False

    def post(self, value, axis, bit, then, rank, weight=1.0):
        line = (axis, bit) if axis == "seq" else (axis, 0)
        size = value.size * value.dtype.itemsize * weight / (RATE * 1e6)
        queue = self.queues.setdefault(line, [])
        queue.append((value, axis, bit, size, then, rank))
        queue.sort(key=lambda entry: entry[-1])
        self.begin()

    def begin(self):
        for line, queue in self.queues.items():
            busy = self.busy.setdefault(line, [])
            depth = self.depth if line[0] == "seq" else 1
            while queue and len(busy) < depth and not (self.held and line[0] == "seq"):
                value, axis, bit, duration, then, _ = queue.pop(0)
                ahead = self.last.get(line, []) + (self.latest if axis == "seq" else [])
                if ahead:
                    value = lax.optimization_barrier((value, ahead))[0]
                self.now += SEND
                start = max([self.now] + [entry[0] for entry in busy])
                busy.append((start + duration, pxor(value, axis, 1 << bit), then))

    def pump(self):
        while True:
            lines = [line for line, busy in self.busy.items() if busy]
            line = min(lines, key=lambda entry: self.busy[entry][0][0], default=None)
            if line is None or self.busy[line][0][0] > self.now:
                break
            _, got, then = self.busy[line].pop(0)
            self.last[line] = [got]
            self.fresh.append(got)
            then(got)
            self.begin()

    def hold(self, cost):
        self.pump()
        self.held = True
        left = [entry[0] for line, busy in self.busy.items() if line[0] == "seq" for entry in busy]
        self.now = max([self.now] + left) + cost

    def release(self, got):
        self.held = False
        self.latest = [got]
        self.begin()
        self.latest = []

    def until(self, ready):
        self.pump()
        while not ready():
            self.now = max(self.now, min(busy[0][0] for busy in self.busy.values() if busy))
            self.pump()

    def step(self, cost, value):
        self.pump()
        if self.before is not None:
            self.fresh.append(self.before)
            self.before = None
        if self.fresh:
            value = lax.optimization_barrier((value, self.fresh))[0]
            self.fresh = []
        self.now += cost * self.scale
        return value

    def note(self, *arrays):
        self.fresh.extend(arrays)

    def ran(self, outputs):
        self.before = outputs[0]
        return outputs


def bits_of(size):
    return max(size.bit_length() - 1, 0)


def pxor(value, axis, flip):
    size = lax.axis_size(axis)
    return lax.ppermute(value, axis, [(i, i ^ flip) for i in range(size)])


def swap(value):
    return pxor(value, "tensor", 1)


def take(value, axis, index):
    return lax.dynamic_index_in_dim(value, index, axis, keepdims=False)


def place_kernel(cuts, idx_ref, *refs):
    inner = len(refs) - len(cuts)
    blocks, outs = refs[:inner], refs[inner:]
    for rel, block in enumerate(blocks):
        at = jnp.bitwise_xor(idx_ref[1], rel)
        for (top, rows, left, cols, before, after), out_ref in zip(cuts, outs):
            part = block[0, top : top + rows, left : left + cols]
            sides = [part]
            if before:
                sides.insert(0, jnp.zeros((rows, before), part.dtype))
            if after:
                sides.append(jnp.zeros((rows, after), part.dtype))
            out_ref[0, at] = jnp.concatenate(sides, axis=1) if len(sides) > 1 else part


def place(blocks, outer_index, inner_index, cuts=None):
    outer, rows, cols = blocks[0].shape
    inner = len(blocks)
    cuts = cuts or ((0, rows, 0, cols, 0, 0),)
    start = jnp.int32(0) if outer_index is None else outer_index
    index = jnp.stack([start, inner_index]).astype(jnp.int32)
    sizes = [(cut[1], cut[3] + cut[4] + cut[5]) for cut in cuts]
    return pl.pallas_call(
        partial(place_kernel, cuts),
        grid_spec=pltpu.PrefetchScalarGridSpec(
            num_scalar_prefetch=1,
            grid=(outer,),
            in_specs=[pl.BlockSpec((1, rows, cols), lambda o, idx: (o, 0, 0))] * inner,
            out_specs=[
                pl.BlockSpec((1, inner) + size, lambda o, idx: (jnp.bitwise_xor(idx[0], o), 0, 0, 0))
                for size in sizes
            ],
        ),
        out_shape=[jax.ShapeDtypeStruct((outer, inner) + size, blocks[0].dtype) for size in sizes],
        compiler_params=pltpu.CompilerParams(vmem_limit_bytes=12 * MIB),
        cost_estimate=LIGHT,
        name="place",
    )(index, *blocks)


class Gather:
    def __init__(self, flow, rank, halves, dp_index, seq_index, cuts, cost):
        self.rank = rank
        self.flow, self.index, self.cuts, self.cost = flow, (dp_index, seq_index), cuts, cost
        self.count, self.outer = bits_of(lax.axis_size("seq")), bits_of(lax.axis_size("dp"))
        self.trees = [{}, {}]
        self.blocks = {}
        self.along_dp((0, 1), 0, self.outer, jnp.stack(halves))

    def along_dp(self, which, rel, below, block):
        blocks = self.blocks.setdefault(which, {})
        blocks[rel] = block
        for bit in reversed(range(below)):
            then = partial(self.along_dp, which, rel | 1 << bit, bit)
            self.flow.post(block, "dp", bit, then, self.rank, 1.0 + bit)
        if len(blocks) == 1 << self.outer:
            ordered = [blocks[r] for r in range(1 << self.outer)]
            for half in which:
                self.flow.now += HALF
                part = ordered if len(which) == 1 else [block[half] for block in ordered]
                self.along_seq(half, 0, 0, jnp.stack(part))

    def along_seq(self, which, rel, first, block):
        self.trees[which][rel] = block
        for step in range(first, self.count):
            bit = step if which == 0 else self.count - 1 - step
            self.flow.post(block, "seq", bit, partial(self.along_seq, which, rel | 1 << bit, step + 1), self.rank)

    def ready(self):
        return all(len(tree) == 1 << self.count for tree in self.trees)

    def result(self):
        self.flow.until(self.ready)
        results = []
        for which in range(2):
            ordered = [self.trees[which][rel] for rel in range(1 << self.count)]
            ordered[0] = self.flow.step(self.cost, ordered[0])
            placed = self.flow.ran(place(ordered, *self.index, self.cuts[which]))
            results.append([p.reshape(-1, p.shape[-1]) for p in placed])
        return results


def add_up(parts):
    return sum(part.astype(f32) for part in parts[1:]) + parts[0].astype(f32)


class Scatter:
    def __init__(self, flow, rank):
        self.flow, self.rank = flow, rank
        self.count, self.outer = bits_of(lax.axis_size("seq")), bits_of(lax.axis_size("dp"))
        self.halves = [None, None]
        self.total = None

    def give(self, which, kept, sent):
        order = list(range(self.count))
        if which == 0:
            order.reverse()
        left = [bit for bit in reversed(range(self.count)) if bit != order[0]]
        shape = kept.shape[:1] + (2,) * (self.count - 1) + kept.shape[2:]
        self.flow.post(
            sent,
            "seq",
            order[0],
            lambda got: self.along_seq(which, order[1:], left, [kept.reshape(shape), got.reshape(shape)]),
            self.rank,
        )

    def split(self, parts, axis, bit, dim):
        mine = (lax.axis_index(axis) >> bit) & 1
        away = add_up([take(part, dim, 1 - mine) for part in parts]).astype(bf16)
        self.flow.note(away)
        kept = add_up([take(part, dim, mine) for part in parts]).astype(bf16)
        return kept, away

    def along_seq(self, which, order, left, parts):
        if not order:
            self.halves[which] = parts
            if all(half is not None for half in self.halves):
                both = [jnp.stack(pair) for pair in zip(*self.halves)]
                both = [v.reshape((2,) + (2,) * self.outer + v.shape[2:]) for v in both]
                self.along_dp(0, both)
            return
        self.flow.now += ADD
        bit = order[0]
        kept, away = self.split(parts, "seq", bit, 1 + left.index(bit))
        rest = [b for b in left if b != bit]
        self.flow.post(away, "seq", bit, lambda got: self.along_seq(which, order[1:], rest, [kept, got]), self.rank)

    def along_dp(self, bit, parts):
        if bit == self.outer:
            self.total = add_up(parts)
            return
        self.flow.now += ADD
        kept, away = self.split(parts, "dp", bit, self.outer - bit)
        self.flow.post(away, "dp", bit, lambda got: self.along_dp(bit + 1, [kept, got]), self.rank, 1.0 + bit)


def scatter_small(value, axis):
    count = bits_of(lax.axis_size(axis))
    value = value.reshape((2,) * count + value.shape[1:])
    for bit in reversed(range(count)):
        mine = (lax.axis_index(axis) >> bit) & 1
        value = take(value, 0, mine) + pxor(take(value, 0, 1 - mine), axis, 1 << bit)
    return value


def sum_small(value, axis):
    for bit in range(bits_of(lax.axis_size(axis))):
        value = value + pxor(value, axis, 1 << bit)
    return value


def gather_small(value, axis):
    for bit in range(bits_of(lax.axis_size(axis))):
        value = jnp.concatenate([value, pxor(value, axis, 1 << bit)], axis=0)
    return value


def dispatch(arrays):
    size, index = lax.axis_size("seq"), lax.axis_index("seq")
    parts = []
    for rel in range(size):
        views = [a.reshape(a.shape[0], size, a.shape[1] // size, a.shape[2]) for a in arrays]
        taken = [take(view, 1, index ^ rel) for view in views]
        part = jnp.concatenate(taken, axis=-1) if len(taken) > 1 else taken[0]
        parts.append(part if rel == 0 else pxor(part, "seq", rel))
    stacked = jnp.stack(parts, axis=1)
    return stacked.reshape(stacked.shape[0], -1, stacked.shape[-1])


def collect(rows, cuts):
    size, index = lax.axis_size("seq"), lax.axis_index("seq")
    parts = rows.reshape(rows.shape[0], size, rows.shape[1] // size, rows.shape[2])
    blocks = []
    for rel in range(size):
        block = parts[:, rel]
        blocks.append(block if rel == 0 else pxor(block, "seq", rel))
    return [p.reshape(-1, p.shape[-1]) for p in place(blocks, None, index, cuts)]


def head_windows(width):
    spans = []
    for first in range(0, width, HEAD_DIM):
        low = first // LANES * LANES
        high = min(-(-(first + HEAD_DIM) // LANES) * LANES, width)
        spans.append((first, low, high))
    return spans


def head_mask(first, low, high):
    lane = lax.broadcasted_iota(jnp.int32, (1, high - low), 1) + low
    return jnp.where((lane >= first) & (lane < first + HEAD_DIM), 1.0, 0.0).astype(bf16)


def row_dot(left, right):
    return lax.dot_general(left, right, (((1,), (1,)), ((), ())), preferred_element_type=f32)


def col_dot(left, right):
    return lax.dot_general(left, right, (((0,), (0,)), ((), ())), preferred_element_type=f32)


def softmax_probs(queries, key_rows, apart):
    scores = row_dot(queries, key_rows) * (HEAD_DIM ** (-0.5))
    if apart is not None:
        scores = jnp.where(apart, -1e30, scores)
    top = jnp.max(scores, axis=-1, keepdims=True)
    weights = jnp.exp(scores - top)
    return weights * (1.0 / jnp.sum(weights, axis=-1, keepdims=True))


def tokens_apart(rows, period):
    if period is None:
        return None
    one = lax.broadcasted_iota(jnp.int32, (rows, rows), 0)
    two = lax.broadcasted_iota(jnp.int32, (rows, rows), 1)
    return lax.rem(one, period) != lax.rem(two, period)


def attend_kernel(period, lead, qk_ref, v_ref, out_ref, acc_ref):
    rows, width = acc_ref.shape
    apart = tokens_apart(rows, period)
    queries, key_rows = qk_ref[0, :, :width], qk_ref[0, :, width : 2 * width]
    value_rows = v_ref[0, :, lead : lead + width]
    acc_ref[...] = jnp.zeros_like(acc_ref)
    for first, low, high in head_windows(width):
        mask = head_mask(first, low, high)
        probs = softmax_probs(queries[:, low:high] * mask, key_rows[:, low:high], apart)
        acc_ref[:, low:high] += jnp.dot(
            probs.astype(bf16), value_rows[:, low:high] * mask, preferred_element_type=f32
        )
    attended = acc_ref[...].astype(bf16)
    before = out_ref.shape[2] - width
    if before:
        attended = jnp.concatenate([jnp.zeros((rows, before), bf16), attended], axis=1)
    out_ref[0] = attended


def attend(qk, values, lead, width, before, period):
    blocks, rows = qk.shape[:2]

    def whole(cols):
        return pl.BlockSpec((1, rows, cols), lambda b: (b, 0, 0))

    return pl.pallas_call(
        partial(attend_kernel, period, lead),
        grid=(blocks,),
        out_shape=jax.ShapeDtypeStruct((blocks, rows, before + width), bf16),
        in_specs=[whole(qk.shape[2]), whole(values.shape[2])],
        out_specs=whole(before + width),
        scratch_shapes=[pltpu.VMEM((rows, width), f32)],
        compiler_params=pltpu.CompilerParams(vmem_limit_bytes=24 * MIB),
        cost_estimate=LIGHT,
        name="attend",
    )(qk, values)


def attend_grad_kernel(period, lead, skip, qk_ref, v_ref, da_ref, *refs):
    outs, sum_ref, (acc_q, acc_k, acc_v) = refs[:-4], refs[-4], refs[-3:]
    rows, width = acc_q.shape
    apart = tokens_apart(rows, period)
    queries, key_rows = qk_ref[0, :, :width], qk_ref[0, :, width : 2 * width]
    value_rows = v_ref[0, :, lead : lead + width]
    grad_att = da_ref[0, :, skip : skip + width]
    factor = HEAD_DIM ** (-0.5)
    for acc in (acc_q, acc_k, acc_v):
        acc[...] = jnp.zeros_like(acc)
    for first, low, high in head_windows(width):
        mask = head_mask(first, low, high)
        q_own = queries[:, low:high] * mask
        k_own = key_rows[:, low:high] * mask
        g_own = grad_att[:, low:high] * mask
        probs = softmax_probs(q_own, k_own, apart)
        grad_probs = row_dot(g_own, value_rows[:, low:high])
        inner = jnp.sum(grad_probs * probs, axis=-1, keepdims=True)
        grad_scores = (probs * (grad_probs - inner)).astype(bf16)
        acc_q[:, low:high] += jnp.dot(grad_scores, k_own, preferred_element_type=f32)
        acc_k[:, low:high] += col_dot(grad_scores, q_own)
        acc_v[:, low:high] += col_dot(probs.astype(bf16), g_own)
    grad_q = (acc_q[...] * factor).astype(bf16)
    outs[0][0, :, :width] = grad_q
    outs[0][0, :, width : 2 * width] = (acc_k[...] * factor).astype(bf16)
    grad_v = acc_v[...].astype(bf16)
    if len(outs) == 1:
        outs[0][0, :, 2 * width :] = grad_v
    else:
        outs[1][0] = jnp.concatenate([grad_v, jnp.zeros_like(grad_v)], axis=1)
    sum_ref[0, 0:1, :] = jnp.sum(grad_q.astype(f32), axis=0, keepdims=True)
    sum_ref[0, 1:2, :] = jnp.sum(grad_v.astype(f32), axis=0, keepdims=True)


def attend_grad(qk, values, lead, grad_att, skip, width, period):
    blocks, rows = qk.shape[:2]

    def whole(cols):
        return pl.BlockSpec((1, rows, cols), lambda b: (b, 0, 0))

    cols = [3 * width] if period else [2 * width, 2 * width]
    return pl.pallas_call(
        partial(attend_grad_kernel, period, lead, skip),
        grid=(blocks,),
        out_shape=[jax.ShapeDtypeStruct((blocks, rows, c), bf16) for c in cols]
        + [jax.ShapeDtypeStruct((blocks, 2, width), f32)],
        in_specs=[whole(qk.shape[2]), whole(values.shape[2]), whole(grad_att.shape[2])],
        out_specs=[whole(c) for c in cols] + [pl.BlockSpec((1, 2, width), lambda b: (b, 0, 0))],
        scratch_shapes=[pltpu.VMEM((rows, width), f32)] * 3,
        compiler_params=pltpu.CompilerParams(vmem_limit_bytes=24 * MIB),
        cost_estimate=LIGHT,
        name="attend_grad",
    )(qk, values, grad_att)


def on_chip():
    return pl.BlockSpec(memory_space=pltpu.VMEM)


def in_place():
    return pl.BlockSpec(memory_space=pl.ANY)


def call(kernel, name, inputs, streamed, outs, scratch=(), limit=24, out_specs=None):
    buffers = [pltpu.VMEM(w.shape, w.dtype) for w in streamed]
    sems = [pltpu.SemaphoreType.DMA((len(streamed),))] if streamed else []
    n_in, n_w, n_out = len(inputs), len(streamed), len(outs)

    def body(*refs):
        ins, away = refs[:n_in], refs[n_in : n_in + n_w]
        results = refs[n_in + n_w : n_in + n_w + n_out]
        rest = refs[n_in + n_w + n_out :]
        here, rest = rest[:n_w], rest[n_w:]
        copies = []
        if n_w:
            sem, rest = rest[0], rest[1:]
            copies = [pltpu.make_async_copy(a, h, sem.at[i]) for i, (a, h) in enumerate(zip(away, here))]
            for copy in copies:
                copy.start()

        def fetch(i):
            copies[i].wait()
            return here[i]

        kernel(ins, fetch, results, rest)

    return pl.pallas_call(
        body,
        out_shape=[jax.ShapeDtypeStruct(shape, dtype) for shape, dtype in outs],
        in_specs=[on_chip()] * n_in + [in_place()] * n_w,
        out_specs=out_specs or [on_chip()] * n_out,
        scratch_shapes=buffers + sems + list(scratch),
        compiler_params=pltpu.CompilerParams(vmem_limit_bytes=limit * MIB),
        cost_estimate=LIGHT,
        name=name,
    )(*inputs, *streamed)


def norm_parts(values):
    average = jnp.mean(values, axis=-1, keepdims=True)
    centered = values - average
    variance = jnp.mean(centered * centered, axis=-1, keepdims=True)
    inverse = lax.rsqrt(variance + EPSILON)
    return centered * inverse, inverse


def both(one, two):
    return jnp.concatenate([one[...], two[...]], axis=0)


def modulated(values, mods_ref, shift, scale):
    normed, _ = norm_parts(values)
    return (normed * (1.0 + mods_ref[scale : scale + 1, :]) + mods_ref[shift : shift + 1, :]).astype(bf16)


def norm_forward(x, mods, shift, scale):
    def kernel(ins, fetch, outs, scratch):
        outs[0][...] = modulated(ins[0][...], ins[1], shift, scale)

    return call(kernel, "norm_forward", [x, mods], [], [(x.shape, bf16)])[0]


def project_heads(normed, w_qk, w_vo, biases, row):
    rows, cols = 2 * normed[0].shape[0], w_qk.shape[1]

    def kernel(ins, fetch, outs, scratch):
        tokens = both(ins[0], ins[1])
        for i in range(2):
            bias = ins[2][row + i : row + i + 1, :]
            outs[i][...] = (jnp.dot(tokens, fetch(i)[...], preferred_element_type=f32) + bias).astype(bf16)

    return call(kernel, "project_heads", [*normed, biases], [w_qk, w_vo], [((rows, cols), bf16)] * 2)


def project_back(pairs, dtype, name):
    rows, cols = pairs[0][0].shape[0] // 2, pairs[0][1].shape[0]
    count = len(pairs)

    def kernel(ins, fetch, outs, scratch):
        out = row_dot(ins[0][...], fetch(0)[...])
        for i in range(1, count):
            out = out + row_dot(ins[i][...], fetch(i)[...])
        outs[0][...] = out[:rows]
        outs[1][...] = out[rows:].astype(dtype)

    return call(
        kernel, name, [p[0] for p in pairs], [p[1] for p in pairs], [((rows, cols), f32), ((rows, cols), dtype)]
    )


def residual(x, own, other, biases, bias_row, mods, gate, following):
    def kernel(ins, fetch, outs, scratch):
        branch = ins[1][...] + ins[2][...].astype(f32) + ins[3][bias_row : bias_row + 1, :]
        value = ins[0][...] + ins[4][gate : gate + 1, :] * branch
        outs[0][...] = branch
        outs[1][...] = value
        if following is None:
            outs[2][...] = value.astype(bf16)
        else:
            outs[2][...] = modulated(value, ins[4], *following)

    return call(
        kernel, "residual", [x, own, other, biases, mods], [], [(x.shape, f32), (x.shape, f32), (x.shape, bf16)]
    )


def gelu_parts(pre):
    inner = jnp.tanh(GELU_C * (pre + 0.044715 * (pre * pre * pre)))
    return inner


def mlp_forward(normed, up_a, up_b, down_a, down_b, biases, row, dtype):
    patches, cols = normed[0].shape[0], up_a.shape[1]
    model = down_a.shape[0]
    rows = 2 * patches

    def kernel(ins, fetch, outs, scratch):
        tokens = both(ins[0], ins[1])
        out = None
        for i in range(2):
            bias = ins[2][row + i : row + i + 1, :]
            pre = jnp.dot(tokens, fetch(2 * i)[...], preferred_element_type=f32) + bias
            outs[i][...] = pre
            hidden = (0.5 * pre * (1.0 + gelu_parts(pre))).astype(bf16)
            outs[2 + i][...] = hidden
            part = row_dot(hidden, fetch(2 * i + 1)[...])
            out = part if out is None else out + part
        outs[4][...] = out[:patches]
        outs[5][...] = out[patches:].astype(dtype)

    return call(
        kernel,
        "mlp_forward",
        [*normed, biases],
        [up_a, down_a, up_b, down_b],
        [((rows, cols), f32)] * 2 + [((rows, cols), bf16)] * 2 + [((patches, model), f32), ((patches, model), dtype)],
        limit=48,
    )


def mlp_up(normed, up_a, up_b, biases, row):
    rows, cols = 2 * normed[0].shape[0], up_a.shape[1]

    def kernel(ins, fetch, outs, scratch):
        tokens = both(ins[0], ins[1])
        for i in range(2):
            bias = ins[2][row + i : row + i + 1, :]
            pre = jnp.dot(tokens, fetch(i)[...], preferred_element_type=f32) + bias
            outs[i][...] = pre
            outs[2 + i][...] = (0.5 * pre * (1.0 + gelu_parts(pre))).astype(bf16)

    return call(
        kernel,
        "mlp_up",
        [*normed, biases],
        [up_a, up_b],
        [((rows, cols), f32)] * 2 + [((rows, cols), bf16)] * 2,
        limit=32,
    )


def mlp_backward(grad, pre, up, down, so_far):
    patches, model = grad[0].shape
    rows, cols = pre.shape
    last = so_far is not None

    def kernel(ins, fetch, outs, scratch):
        tokens = both(ins[0], ins[1])
        grad_hidden = jnp.dot(tokens, fetch(0)[...], preferred_element_type=f32)
        value = fetch(1)[...]
        inner = gelu_parts(value)
        slope = 0.5 * (1.0 + inner) + 0.5 * value * (1.0 - inner * inner) * (
            GELU_C * (1.0 + 3.0 * 0.044715 * (value * value))
        )
        grad_pre = (grad_hidden * slope).astype(bf16)
        outs[0][...] = grad_pre
        outs[1][0:1, :] = jnp.sum(grad_pre.astype(f32), axis=0, keepdims=True)
        outs[1][1:2, :] = jnp.sum(tokens.astype(f32), axis=0, keepdims=True)
        out = row_dot(grad_pre, fetch(2)[...])
        if last:
            out = out + fetch(3)[...]
            outs[2][...] = out[:patches]
            outs[3][...] = out[patches:].astype(bf16)
        else:
            outs[2][...] = out

    tail = [((patches, model), f32), ((patches, model), bf16)] if last else [((rows, model), f32)]
    return call(
        kernel,
        "mlp_backward",
        list(grad),
        [down, pre, up] + ([so_far] if last else []),
        [((rows, cols), bf16), ((2, cols), f32)] + tail,
        limit=32,
    )


def grad_heads(grad, w_vo):
    patches, model = grad[0].shape
    cols = w_vo.shape[1]

    def kernel(ins, fetch, outs, scratch):
        tokens = both(ins[0], ins[1])
        outs[1][...] = jnp.sum(tokens.astype(f32), axis=0, keepdims=True)
        outs[0][...] = jnp.dot(tokens, fetch(0)[...], preferred_element_type=f32).astype(bf16)

    return call(kernel, "grad_heads", list(grad), [w_vo], [((2 * patches, cols), bf16), ((1, model), f32)])


def norm_backward(g, own, other, x, mods, scale, gate, branch):
    rows, model = x.shape

    def kernel(ins, fetch, outs, scratch):
        grad = ins[1][...] + ins[2][...].astype(f32)
        normed, inverse = norm_parts(ins[3][...])
        scaled = grad * (1.0 + ins[4][scale : scale + 1, :])
        mean_one = jnp.mean(scaled, axis=-1, keepdims=True)
        mean_two = jnp.mean(scaled * normed, axis=-1, keepdims=True)
        value = ins[0][...] + inverse * (scaled - mean_one - normed * mean_two)
        outs[0][...] = value
        outs[1][0:1, :] = jnp.sum(grad, axis=0, keepdims=True)
        outs[1][1:2, :] = jnp.sum(grad * normed, axis=0, keepdims=True)
        if gate is not None:
            outs[1][2:3, :] = jnp.sum(value * ins[5][...], axis=0, keepdims=True)
            outs[2][...] = (ins[4][gate : gate + 1, :] * value).astype(bf16)

    inputs = [g, own, other, x, mods] + ([] if gate is None else [branch])
    outs = [(x.shape, f32), ((3, model), f32)] + ([] if gate is None else [(x.shape, bf16)])
    return call(kernel, "norm_backward", inputs, [], outs)


def insert_bit(rest, bit):
    low = rest & ((1 << bit) - 1)
    return (rest - low) * 2 + low


def weight_grad(pairs, bit, name):
    clusters, parts = lax.axis_size("dp"), lax.axis_size("seq")
    model, cols = pairs[0][0].shape[1], pairs[0][1].shape[1]
    rows = model // (clusters * parts)
    mine = ((lax.axis_index("seq") >> bit) & 1).astype(jnp.int32).reshape(1)
    shape = (clusters, parts // 2, rows, cols)
    count = len(pairs)

    def body(mine_ref, *refs):
        ins, outs, (whole, sem) = refs[: 2 * count], refs[2 * count : 2 * count + 2], refs[2 * count + 2 :]
        out = col_dot(ins[0][...], ins[1][...])
        for i in range(1, count):
            out = out + col_dot(ins[2 * i][...], ins[2 * i + 1][...])
        copies = []
        for c in range(clusters):
            for part in range(parts):
                at = (c * parts + part) * rows
                whole[c * parts + part] = out[at : at + rows].astype(bf16)
        for c in range(clusters):
            for rest in range(parts // 2):
                start = c * parts + insert_bit(rest, bit)
                for which in range(2):
                    side = mine_ref[0] if which == 0 else 1 - mine_ref[0]
                    copy = pltpu.make_async_copy(
                        whole.at[start + (side << bit)],
                        outs[which].at[c, rest],
                        sem.at[(c * (parts // 2) + rest) * 2 + which],
                    )
                    copy.start()
                    copies.append(copy)
        for copy in copies:
            copy.wait()

    return pl.pallas_call(
        body,
        out_shape=[jax.ShapeDtypeStruct(shape, bf16)] * 2,
        in_specs=[pl.BlockSpec(memory_space=pltpu.SMEM)] + [on_chip()] * (2 * count),
        out_specs=[in_place()] * 2,
        scratch_shapes=[
            pltpu.VMEM((clusters * parts, rows, cols), bf16),
            pltpu.SemaphoreType.DMA((clusters * parts,)),
        ],
        compiler_params=pltpu.CompilerParams(vmem_limit_bytes=32 * MIB),
        cost_estimate=LIGHT,
        name=name,
    )(mine, *[array for pair in pairs for array in pair])


def with_other(flow, own):
    flow.now += SWAP
    return own, swap(own)


def dispatch_in(flow, arrays, cost, hold):
    arrays[0] = flow.step(2.0, arrays[0])
    if hold:
        flow.hold(cost)
        result = dispatch(arrays)
        flow.release(result)
        return result
    flow.now += 2.5 * cost
    return dispatch(arrays)


def collect_in(flow, rows, cuts, cost, hold):
    rows = flow.step(2.0, rows)
    if hold:
        flow.hold(cost)
        result = collect(rows, cuts)
        flow.release(result[0])
        return result
    flow.now += 2.5 * cost
    return collect(rows, cuts)


def layer_forward(flow, x, normed_one, mods, layer, units, biases_of, temporal, following):
    attention_unit, mlp_unit = units
    patches = x.shape[0]
    base = 6 * layer
    normed_one = with_other(flow, normed_one)
    w_qk, w_vo = attention_unit()
    width = w_qk.shape[1] // 2
    biases = biases_of()
    qk, vo = flow.ran(project_heads((flow.step(6.5, normed_one[0]), normed_one[1]), w_qk, w_vo, biases, base))
    qk = qk.reshape(2, patches, -1)
    vo = vo.reshape(2, patches, -1)
    if temporal:
        period = patches // lax.axis_size("seq")
        qkv = dispatch_in(flow, [qk, vo[:, :, :width]], 17.0 * TRIP, False)
        heads = (flow.step(3.5, qkv), qkv, 2 * width)
        attended = attend(*heads, width, 0, period)
        attended = collect_in(flow, attended, ((0, period, 0, width, width, 0),), 11.0 * TRIP, False)[0]
    else:
        heads = (flow.step(3.5, qk), vo, 0)
        attended = attend(*heads, width, width, None).reshape(2 * patches, -1)
    own, other = flow.ran(project_back([(flow.step(2.5, attended), w_vo)], f32, "project_out"))
    other = swap(other)
    flow.now += SWAP
    branch, x_mid, normed_two = flow.ran(
        residual(x, flow.step(2.0, own), other, biases, base + 2, mods, base + 2, (base + 3, base + 4))
    )
    normed_two = with_other(flow, normed_two)
    if following is not None:
        w_up_a, w_down_a, w_up_b, w_down_b = mlp_unit()
        tokens = (flow.step(11.0, normed_two[0]), normed_two[1])
        pre_a, pre_b, hidden_a, hidden_b, own, other = flow.ran(
            mlp_forward(tokens, w_up_a, w_up_b, w_down_a, w_down_b, biases, base + 3, f32)
        )
        other = swap(other)
        flow.now += SWAP
        mlp, x_next, after = flow.ran(
            residual(x_mid, flow.step(2.0, own), other, biases, base + 5, mods, base + 5, following)
        )
        finish = None
        downs = (w_down_a, w_down_b)
    else:
        w_up_a, w_down_a, w_up_b, w_down_b = mlp_unit()
        tokens = (flow.step(8.0, normed_two[0]), normed_two[1])
        pre_a, pre_b, hidden_a, hidden_b = flow.ran(mlp_up(tokens, w_up_a, w_up_b, biases, base + 3))
        downs = (w_down_a, w_down_b)
        mlp = x_next = after = None

        def finish(down_a, down_b):
            first = flow.step(4.0, hidden_a)
            own, other = flow.ran(project_back([(first, down_a), (hidden_b, down_b)], f32, "project_down"))
            other = swap(other)

            def rest():
                return flow.ran(residual(x_mid, flow.step(2.0, own), other, biases, base + 5, mods, base + 5, None))

            return rest

    saved = (x, normed_one, heads, attended, branch, x_mid, normed_two, pre_a, pre_b, hidden_a, hidden_b, mlp)
    weights = (w_qk, w_vo, w_up_a, w_up_b, downs)
    return x_next, after, saved, weights, finish


def layer_backward(flow, g, grad_mlp, mods, layer, weights, saved, temporal, below, finish):
    w_qk, w_vo, w_up_a, w_up_b, downs = weights
    x, normed_one, heads, attended, branch, x_mid, normed_two, pre_a, pre_b, hidden_a, hidden_b, _ = saved
    patches = x.shape[0]
    width = w_qk.shape[1] // 2
    base = 6 * layer
    done = [Scatter(flow, 20 - 4 * layer - unit) for unit in range(3)]
    bits = (bits_of(lax.axis_size("seq")) - 1, 0)

    def reduce_half(unit, which, pairs, name):
        first = flow.step(5.0, pairs[0][1])
        done[unit].give(which, *flow.ran(weight_grad([(pairs[0][0], first)] + pairs[1:], bits[which], name)))

    def joined(pair):
        return jnp.concatenate(pair, axis=0)

    grad_mlp = with_other(flow, grad_mlp)
    grad_mlp_rows = joined(grad_mlp)
    reduce_half(2, 0, [(grad_mlp_rows, hidden_a)], "down_grad")
    reduce_half(2, 1, [(grad_mlp_rows, hidden_b)], "down_grad")
    w_down_a, w_down_b = downs
    normed_rows = joined(normed_two)
    tokens = (flow.step(7.0, grad_mlp[0]), grad_mlp[1])
    grad_pre_a, sums_a, so_far = flow.ran(mlp_backward(tokens, pre_a, w_up_a, w_down_a, None))
    reduce_half(1, 0, [(normed_rows, grad_pre_a)], "up_grad")
    tokens = (flow.step(8.0, grad_mlp[0]), grad_mlp[1])
    grad_pre_b, sums_b, own, other = flow.ran(mlp_backward(tokens, pre_b, w_up_b, w_down_b, so_far))
    other = swap(other)
    reduce_half(1, 1, [(normed_rows, grad_pre_b)], "up_grad")
    g_mid, sums_two, grad_branch = flow.ran(
        norm_backward(g, flow.step(2.0, own), other, x_mid, mods, base + 4, base + 2, branch)
    )
    other_branch = swap(grad_branch)
    flow.now += 4.0
    grad_branch = (flow.step(2.5, grad_branch), other_branch)
    grad_att, sum_branch = flow.ran(grad_heads(grad_branch, w_vo))
    grad_att = grad_att.reshape(2, patches, -1)
    rest = finished = None
    if finish is not None:
        rest = finish(w_down_a, w_down_b)
    if temporal:
        period = patches // lax.axis_size("seq")
        grad_att = dispatch_in(flow, [grad_att[:, :, width:]], 10.0 * TRIP, HOLD)
        grad_qkv, sums_pair = flow.ran(attend_grad(*heads, flow.step(10.5, grad_att), 0, width, period))
        cuts = ((0, period, 0, 2 * width, 0, 0), (0, period, 2 * width, width, 0, width))
        grad_qk, grad_v = collect_in(flow, grad_qkv, cuts, 18.0 * TRIP, HOLD)
    else:
        grad_qk, grad_v, sums_pair = flow.ran(
            attend_grad(*heads, flow.step(10.5, grad_att), width, width, None)
        )
        grad_qk = grad_qk.reshape(2 * patches, -1)
        grad_v = grad_v.reshape(2 * patches, -1)
    if rest is not None:
        finished = rest()
    own, other = flow.ran(
        project_back([(flow.step(5.0, grad_qk), w_qk), (grad_v, w_vo)], bf16, "grad_normed")
    )
    other = swap(other)
    rows_one = joined(normed_one)
    reduce_half(0, 0, [(rows_one, grad_qk)], "heads_grad")
    own = flow.step(2.0, own)
    if below is None:
        g_below, sums_one = flow.ran(norm_backward(g_mid, own, other, x, mods, base + 1, None, None))
        grad_below = None
    else:
        g_below, sums_one, grad_below = flow.ran(
            norm_backward(g_mid, own, other, x, mods, base + 1, base - 1, below)
        )
    reduce_half(0, 1, [(rows_one, grad_v), (joined(grad_branch), attended)], "heads_grad")
    mod_sums = [sums_one[0], sums_one[1], sums_two[2], sums_two[0], sums_two[1]]
    bias_sums = [
        jnp.sum(sums_pair, axis=0).reshape(-1),
        sum_branch.reshape(-1),
        sums_a[0],
        sums_b[0],
        sums_a[1],
    ]
    return g_below, grad_below, mod_sums, sums_one[2], bias_sums, done, finished


def shards(
    tokens,
    conditioning,
    cotangent,
    modulation_weight,
    modulation_bias,
    triple_weight,
    pair_bias,
    out_weight,
    out_bias,
    hidden_weight,
    hidden_bias,
    output_weight,
    output_bias,
):
    layers, _, _, width = triple_weight.shape
    model = tokens.shape[3]
    patches = tokens.shape[2]
    own_clips = tokens.shape[0] // lax.axis_size("tensor")
    all_clips = conditioning.shape[0]
    assert own_clips == 1 and tokens.shape[1] == 1 and layers == 2
    assert model == 2 * width and hidden_weight.shape[2] == 2 * model
    units = hidden_weight.shape[2]
    half = units // 2
    dp_index, seq_index = lax.axis_index("dp"), lax.axis_index("seq")
    core = lax.axis_index("tensor")
    n_dp, n_seq, n_core = lax.axis_size("dp"), lax.axis_size("seq"), lax.axis_size("tensor")

    packed = jnp.concatenate(
        [pair_bias.reshape(layers, -1), out_bias, hidden_bias.reshape(layers, -1), output_bias], axis=1
    ).reshape(-1)
    rows = triple_weight.shape[1]

    def attention_unit(layer):
        triple = triple_weight[layer]
        first = jnp.concatenate([triple[:, 0], triple[:, 1]], axis=1)
        second = jnp.concatenate([triple[:, 2], out_weight[layer].T], axis=1)
        if layer == 0:
            extra = jnp.zeros((8 * 2 * width,), bf16).at[: packed.shape[0]].set(packed).reshape(8, -1)
            first = jnp.concatenate([first, extra])
            second = jnp.concatenate([second, jnp.zeros_like(extra)])
        return first, second

    def mlp_unit(layer):
        down = output_weight[layer].T
        up = hidden_weight[layer]
        parts = (slice(0, half), slice(half, None))
        return [[jnp.concatenate([up[:, part], down[:, part]], axis=1) for part in parts]]

    flow = Flow()
    flow.now = 8.0
    gathers = []
    for layer in range(layers):
        whole = (0, rows, 0, 2 * width, 0, 0)
        first_cuts = (whole, (rows, 8, 0, 2 * width, 0, 0)) if layer == 0 else (whole,)
        attention = Gather(flow, 2 * layer, attention_unit(layer), dp_index, seq_index, (first_cuts, (whole,)), 2.0)
        pair_cuts = ((0, rows, 0, half, 0, 0), (0, rows, half, half, 0, 0))
        mlp = mlp_unit(layer)
        mlp_cuts = (pair_cuts, pair_cuts) if len(mlp) == 1 else ((whole,), (whole,))
        mlp = [
            Gather(flow, 2 * layer + 1 + i, halves, dp_index, seq_index, mlp_cuts, 3.5 if len(mlp) == 1 else 2.0)
            for i, halves in enumerate(mlp)
        ]
        gathers.append((attention, mlp))

    act_cond, silu_back = jax.vjp(jax.nn.silu, conditioning)
    act_low = act_cond.astype(bf16)
    local_term = jnp.einsum("cd,lde->cle", act_low, modulation_weight, preferred_element_type=f32)
    bias_cols = modulation_bias.shape[1]
    offset = ((dp_index * n_seq + seq_index) * n_core + core) * bias_cols
    bias_full = lax.dynamic_update_slice(
        jnp.zeros((layers, local_term.shape[2]), f32), modulation_bias.astype(f32), (jnp.int32(0), offset)
    )
    contribution = (local_term + bias_full[None]).reshape(n_dp, n_core, -1)
    contribution = take(contribution, 1, core) + swap(take(contribution, 1, 1 - core))
    contribution = flow.step(25.0, contribution)
    mods = sum_small(scatter_small(contribution, "dp"), "seq").reshape(layers * 6, model)

    def unpack(spread):
        spread = spread.reshape(n_dp * n_seq, -1)[:, : packed.shape[0]].reshape(n_dp * n_seq, layers, -1)
        spread = spread.transpose(1, 0, 2).astype(f32)
        cuts, at = [], 0
        for size in (pair_bias.shape[3], pair_bias.shape[3], out_bias.shape[1], hidden_bias.shape[2], output_bias.shape[1]):
            cuts.append(spread[:, :, at : at + size].reshape(layers, -1))
            at += size
        blank = jnp.zeros_like(cuts[0])
        return jnp.concatenate([cuts[0], blank, cuts[1], blank, *cuts[2:]], axis=1).reshape(6 * layers, model)

    found = {}

    def attention_weights(layer):
        first, second = gathers[layer][0].result()
        if layer == 0:
            found["biases"] = unpack(first[1])
        return first[0], second[0]

    def mlp_weights(layer):
        first, second = gathers[layer][1][0].result()
        return first + second

    x = take(tokens, 0, core).reshape(patches, model).astype(f32)
    after = norm_forward(x, mods, 0, 1)
    kept, weights = [], []
    for layer in range(layers):
        following = (6 * layer + 6, 6 * layer + 7) if layer + 1 < layers else None
        pending = (partial(attention_weights, layer), partial(mlp_weights, layer))
        x, after, saved, layer_weights, finish = layer_forward(
            flow, x, after, mods, layer, pending, lambda: found["biases"], layer == 1, following
        )
        kept.append(saved)
        weights.append(layer_weights)

    def to_both(own):
        other = swap(own)
        pair = jnp.stack([jnp.where(core == 0, own, other), jnp.where(core == 0, other, own)])
        return pair.reshape((2, 1) + own.shape)

    g = take(cotangent, 0, core).reshape(patches, model).astype(f32)
    grad_mlp = (mods[6 * layers - 1] * g).astype(bf16)
    grad_gates = [None] * layers
    top = g
    mod_grads, bias_grads, done = [None] * layers, [None] * layers, [None] * layers
    flow.depth, flow.scale = DEPTH, SCALE_B
    for layer in reversed(range(layers)):
        below = kept[layer - 1][-1] if layer else None
        g, grad_mlp, mod_sums, grad_gate, bias_grads[layer], done[layer], finished = layer_backward(
            flow, g, grad_mlp, mods, layer, weights[layer], kept[layer], layer == 1, below, finish
        )
        if finished is not None:
            grad_gates[layer] = jnp.sum(top * finished[0], axis=0)
            activations = to_both(finished[2])
            finish = None
        mod_grads[layer] = jnp.concatenate(mod_sums + [grad_gates[layer]])
        if layer:
            grad_gates[layer - 1] = grad_gate
    input_grad = to_both(g)
    flow.until(lambda: all(unit.total is not None for layer in range(layers) for unit in done[layer]))

    def stack_layers(which, build):
        return jnp.stack([build(done[layer][which].total) for layer in range(layers)])

    triple_grad = stack_layers(
        0, lambda u: jnp.stack([u[0][:, :width], u[0][:, width:], u[1][:, :width]], axis=1)
    )
    out_grad = stack_layers(0, lambda u: u[1][:, width:].T)
    hidden_grad = stack_layers(1, lambda u: jnp.concatenate([u[0], u[1]], axis=1))
    output_grad = stack_layers(2, lambda u: jnp.concatenate([u[0], u[1]], axis=1).T)

    flat = [part for layer in range(layers) for part in bias_grads[layer]]
    summed = sum_small(jnp.concatenate(mod_grads + flat), "seq").astype(bf16)
    mods_size = 6 * model * layers
    pair = jnp.concatenate([summed[:mods_size], swap(summed[:mods_size]), summed[mods_size:]])
    spread = gather_small(pair.reshape(1, -1, 128), "dp").reshape(n_dp, -1)
    spread = [spread[rel] for rel in range(n_dp)]
    grad_mods = jnp.stack([s[c * mods_size : (c + 1) * mods_size] for s in spread for c in range(n_core)])
    grad_mods = grad_mods.reshape(all_clips, layers, -1)
    clip = jnp.arange(all_clips)
    clip = (clip // n_core ^ dp_index) * n_core + (clip % n_core ^ core)
    bias_sums = add_up([s[n_core * mods_size :] for s in spread]).reshape(layers, -1)
    owner = dp_index * n_seq + seq_index
    bias_out, at = [], 0
    for size, shape in (
        (width, None),
        (width, None),
        (model, out_bias.shape),
        (units, hidden_bias.shape),
        (model, output_bias.shape),
    ):
        part = bias_sums[:, at : at + size].reshape(layers, n_dp * n_seq, -1)
        part = take(part, 1, owner)
        bias_out.append(part if shape is None else part.reshape(shape))
        at += size
    pair_out = jnp.stack(bias_out[:2], axis=1).reshape(pair_bias.shape)
    out_bias_grad, hidden_bias_grad, output_bias_grad = bias_out[2:]
    modulation_weight_grad = jnp.einsum("cd,cle->lde", act_low[clip], grad_mods, preferred_element_type=f32)
    modulation_bias_grad = lax.dynamic_slice_in_dim(
        jnp.sum(grad_mods, axis=0, dtype=f32), offset, bias_cols, 1
    )
    grad_act = jnp.einsum("cle,lde->cd", grad_mods, modulation_weight, preferred_element_type=f32)
    cond_grad = silu_back(grad_act[clip])[0]
    return (
        activations,
        input_grad,
        cond_grad,
        modulation_weight_grad,
        modulation_bias_grad,
        triple_grad,
        pair_out,
        out_grad,
        out_bias_grad,
        hidden_grad,
        hidden_bias_grad,
        output_grad,
        output_bias_grad,
    )


def solution(mesh):
    owners = ("dp", "seq")
    everyone = ("dp", "seq", "tensor")
    rows = P("dp", "seq", None, None)
    weights = (
        P(None, everyone, None),
        P(None, everyone),
        P(None, owners, None, "tensor"),
        P(None, None, "tensor", owners),
        P(None, "tensor", owners),
        P(None, owners),
        P(None, owners, "tensor"),
        P(None, "tensor", owners),
        P(None, "tensor", owners),
        P(None, owners),
    )
    return jax.shard_map(
        shards,
        mesh=mesh,
        in_specs=(rows, P(None, everyone), rows) + weights,
        out_specs=(rows, rows, P(None, everyone)) + weights,
        check_vma=False,
    )
```

```python
from functools import partial

import jax
import jax.numpy as jnp
from jax import lax
from jax.experimental import pallas as pl
from jax.experimental.pallas import tpu as pltpu
from jax.sharding import PartitionSpec as P

HEAD_DIM = 72
LANES = 128
EPSILON = 1e-06
MIB = 1024 * 1024
SCALE = 1.12
SCALE_B = 1.05
TRIP = 1.13
ADD = 4.0
SWAP = 8.0
RATE = 0.0392
SEND = 0.5
DEPTH = 2
HOLD = True
HALF = 0.0
f32 = jnp.float32
bf16 = jnp.bfloat16
LIGHT = pl.CostEstimate(flops=1, bytes_accessed=1, transcendentals=0)
GELU_C = 0.7978845608028654


class Flow:
    def __init__(self):
        self.now = 0.0
        self.busy = {}
        self.queues = {}
        self.fresh = []
        self.before = None
        self.latest = []
        self.last = {}
        self.depth = 1
        self.scale = SCALE
        self.held = False

    def post(self, value, axis, bit, then, rank, weight=1.0):
        line = (axis, bit) if axis == "seq" else (axis, 0)
        size = value.size * value.dtype.itemsize * weight / (RATE * 1e6)
        queue = self.queues.setdefault(line, [])
        queue.append((value, axis, bit, size, then, rank))
        queue.sort(key=lambda entry: entry[-1])
        self.begin()

    def begin(self):
        for line, queue in self.queues.items():
            busy = self.busy.setdefault(line, [])
            depth = self.depth if line[0] == "seq" else 1
            while queue and len(busy) < depth and not (self.held and line[0] == "seq"):
                value, axis, bit, duration, then, _ = queue.pop(0)
                ahead = self.last.get(line, []) + (self.latest if axis == "seq" else [])
                if ahead:
                    value = lax.optimization_barrier((value, ahead))[0]
                self.now += SEND
                start = max([self.now] + [entry[0] for entry in busy])
                busy.append((start + duration, pxor(value, axis, 1 << bit), then))

    def pump(self):
        while True:
            lines = [line for line, busy in self.busy.items() if busy]
            line = min(lines, key=lambda entry: self.busy[entry][0][0], default=None)
            if line is None or self.busy[line][0][0] > self.now:
                break
            _, got, then = self.busy[line].pop(0)
            self.last[line] = [got]
            self.fresh.append(got)
            then(got)
            self.begin()

    def hold(self, cost):
        self.pump()
        self.held = True
        left = [entry[0] for line, busy in self.busy.items() if line[0] == "seq" for entry in busy]
        self.now = max([self.now] + left) + cost

    def release(self, got):
        self.held = False
        self.latest = [got]
        self.begin()
        self.latest = []

    def until(self, ready):
        self.pump()
        while not ready():
            self.now = max(self.now, min(busy[0][0] for busy in self.busy.values() if busy))
            self.pump()

    def step(self, cost, value):
        self.pump()
        if self.before is not None:
            self.fresh.append(self.before)
            self.before = None
        if self.fresh:
            value = lax.optimization_barrier((value, self.fresh))[0]
            self.fresh = []
        self.now += cost * self.scale
        return value

    def note(self, *arrays):
        self.fresh.extend(arrays)

    def ran(self, outputs):
        self.before = outputs[0]
        return outputs


def bits_of(size):
    return max(size.bit_length() - 1, 0)


def pxor(value, axis, flip):
    size = lax.axis_size(axis)
    return lax.ppermute(value, axis, [(i, i ^ flip) for i in range(size)])


def swap(value):
    return pxor(value, "tensor", 1)


def take(value, axis, index):
    return lax.dynamic_index_in_dim(value, index, axis, keepdims=False)


def place_kernel(cuts, idx_ref, *refs):
    inner = len(refs) - len(cuts)
    blocks, outs = refs[:inner], refs[inner:]
    for rel, block in enumerate(blocks):
        at = jnp.bitwise_xor(idx_ref[1], rel)
        for (top, rows, left, cols, before, after), out_ref in zip(cuts, outs):
            part = block[0, top : top + rows, left : left + cols]
            sides = [part]
            if before:
                sides.insert(0, jnp.zeros((rows, before), part.dtype))
            if after:
                sides.append(jnp.zeros((rows, after), part.dtype))
            out_ref[0, at] = jnp.concatenate(sides, axis=1) if len(sides) > 1 else part


def place(blocks, outer_index, inner_index, cuts=None):
    outer, rows, cols = blocks[0].shape
    inner = len(blocks)
    cuts = cuts or ((0, rows, 0, cols, 0, 0),)
    start = jnp.int32(0) if outer_index is None else outer_index
    index = jnp.stack([start, inner_index]).astype(jnp.int32)
    sizes = [(cut[1], cut[3] + cut[4] + cut[5]) for cut in cuts]
    return pl.pallas_call(
        partial(place_kernel, cuts),
        grid_spec=pltpu.PrefetchScalarGridSpec(
            num_scalar_prefetch=1,
            grid=(outer,),
            in_specs=[pl.BlockSpec((1, rows, cols), lambda o, idx: (o, 0, 0))] * inner,
            out_specs=[
                pl.BlockSpec((1, inner) + size, lambda o, idx: (jnp.bitwise_xor(idx[0], o), 0, 0, 0))
                for size in sizes
            ],
        ),
        out_shape=[jax.ShapeDtypeStruct((outer, inner) + size, blocks[0].dtype) for size in sizes],
        compiler_params=pltpu.CompilerParams(vmem_limit_bytes=12 * MIB),
        cost_estimate=LIGHT,
        name="place",
    )(index, *blocks)


class Gather:
    def __init__(self, flow, rank, halves, dp_index, seq_index, cuts, cost):
        self.rank = rank
        self.flow, self.index, self.cuts, self.cost = flow, (dp_index, seq_index), cuts, cost
        self.count, self.outer = bits_of(lax.axis_size("seq")), bits_of(lax.axis_size("dp"))
        self.trees = [{}, {}]
        self.blocks = {}
        self.along_dp((0, 1), 0, self.outer, jnp.stack(halves))

    def along_dp(self, which, rel, below, block):
        blocks = self.blocks.setdefault(which, {})
        blocks[rel] = block
        for bit in reversed(range(below)):
            then = partial(self.along_dp, which, rel | 1 << bit, bit)
            self.flow.post(block, "dp", bit, then, self.rank, 1.0 + bit)
        if len(blocks) == 1 << self.outer:
            ordered = [blocks[r] for r in range(1 << self.outer)]
            for half in which:
                self.flow.now += HALF
                part = ordered if len(which) == 1 else [block[half] for block in ordered]
                self.along_seq(half, 0, 0, jnp.stack(part))

    def along_seq(self, which, rel, first, block):
        self.trees[which][rel] = block
        for step in range(first, self.count):
            bit = step if which == 0 else self.count - 1 - step
            self.flow.post(block, "seq", bit, partial(self.along_seq, which, rel | 1 << bit, step + 1), self.rank)

    def ready(self):
        return all(len(tree) == 1 << self.count for tree in self.trees)

    def result(self):
        self.flow.until(self.ready)
        results = []
        for which in range(2):
            ordered = [self.trees[which][rel] for rel in range(1 << self.count)]
            ordered[0] = self.flow.step(self.cost, ordered[0])
            placed = self.flow.ran(place(ordered, *self.index, self.cuts[which]))
            results.append([p.reshape(-1, p.shape[-1]) for p in placed])
        return results


def add_up(parts):
    return sum(part.astype(f32) for part in parts[1:]) + parts[0].astype(f32)


class Scatter:
    def __init__(self, flow, rank):
        self.flow, self.rank = flow, rank
        self.count, self.outer = bits_of(lax.axis_size("seq")), bits_of(lax.axis_size("dp"))
        self.halves = [None, None]
        self.total = None

    def give(self, which, kept, sent):
        order = list(range(self.count))
        if which == 0:
            order.reverse()
        left = [bit for bit in reversed(range(self.count)) if bit != order[0]]
        shape = kept.shape[:1] + (2,) * (self.count - 1) + kept.shape[2:]
        self.flow.post(
            sent,
            "seq",
            order[0],
            lambda got: self.along_seq(which, order[1:], left, [kept.reshape(shape), got.reshape(shape)]),
            self.rank,
        )

    def split(self, parts, axis, bit, dim):
        mine = (lax.axis_index(axis) >> bit) & 1
        away = add_up([take(part, dim, 1 - mine) for part in parts]).astype(bf16)
        self.flow.note(away)
        kept = add_up([take(part, dim, mine) for part in parts]).astype(bf16)
        return kept, away

    def along_seq(self, which, order, left, parts):
        if not order:
            self.halves[which] = parts
            if all(half is not None for half in self.halves):
                both = [jnp.stack(pair) for pair in zip(*self.halves)]
                both = [v.reshape((2,) + (2,) * self.outer + v.shape[2:]) for v in both]
                self.along_dp(0, both)
            return
        self.flow.now += ADD
        bit = order[0]
        kept, away = self.split(parts, "seq", bit, 1 + left.index(bit))
        rest = [b for b in left if b != bit]
        self.flow.post(away, "seq", bit, lambda got: self.along_seq(which, order[1:], rest, [kept, got]), self.rank)

    def along_dp(self, bit, parts):
        if bit == self.outer:
            self.total = add_up(parts)
            return
        self.flow.now += ADD
        kept, away = self.split(parts, "dp", bit, self.outer - bit)
        self.flow.post(away, "dp", bit, lambda got: self.along_dp(bit + 1, [kept, got]), self.rank, 1.0 + bit)


def scatter_small(value, axis):
    count = bits_of(lax.axis_size(axis))
    value = value.reshape((2,) * count + value.shape[1:])
    for bit in reversed(range(count)):
        mine = (lax.axis_index(axis) >> bit) & 1
        value = take(value, 0, mine) + pxor(take(value, 0, 1 - mine), axis, 1 << bit)
    return value


def sum_small(value, axis):
    for bit in range(bits_of(lax.axis_size(axis))):
        value = value + pxor(value, axis, 1 << bit)
    return value


def gather_small(value, axis):
    for bit in range(bits_of(lax.axis_size(axis))):
        value = jnp.concatenate([value, pxor(value, axis, 1 << bit)], axis=0)
    return value


def dispatch(arrays):
    size, index = lax.axis_size("seq"), lax.axis_index("seq")
    parts = []
    for rel in range(size):
        views = [a.reshape(a.shape[0], size, a.shape[1] // size, a.shape[2]) for a in arrays]
        taken = [take(view, 1, index ^ rel) for view in views]
        part = jnp.concatenate(taken, axis=-1) if len(taken) > 1 else taken[0]
        parts.append(part if rel == 0 else pxor(part, "seq", rel))
    stacked = jnp.stack(parts, axis=1)
    return stacked.reshape(stacked.shape[0], -1, stacked.shape[-1])


def collect(rows, cuts):
    size, index = lax.axis_size("seq"), lax.axis_index("seq")
    parts = rows.reshape(rows.shape[0], size, rows.shape[1] // size, rows.shape[2])
    blocks = []
    for rel in range(size):
        block = parts[:, rel]
        blocks.append(block if rel == 0 else pxor(block, "seq", rel))
    return [p.reshape(-1, p.shape[-1]) for p in place(blocks, None, index, cuts)]


def head_windows(width):
    spans = []
    for first in range(0, width, HEAD_DIM):
        low = first // LANES * LANES
        high = min(-(-(first + HEAD_DIM) // LANES) * LANES, width)
        spans.append((first, low, high))
    return spans


def head_mask(first, low, high):
    lane = lax.broadcasted_iota(jnp.int32, (1, high - low), 1) + low
    return jnp.where((lane >= first) & (lane < first + HEAD_DIM), 1.0, 0.0).astype(bf16)


def row_dot(left, right):
    return lax.dot_general(left, right, (((1,), (1,)), ((), ())), preferred_element_type=f32)


def col_dot(left, right):
    return lax.dot_general(left, right, (((0,), (0,)), ((), ())), preferred_element_type=f32)


def softmax_probs(queries, key_rows, apart):
    scores = row_dot(queries, key_rows) * (HEAD_DIM ** (-0.5))
    if apart is not None:
        scores = jnp.where(apart, -1e30, scores)
    top = jnp.max(scores, axis=-1, keepdims=True)
    weights = jnp.exp(scores - top)
    return weights * (1.0 / jnp.sum(weights, axis=-1, keepdims=True))


def tokens_apart(rows, period):
    if period is None:
        return None
    one = lax.broadcasted_iota(jnp.int32, (rows, rows), 0)
    two = lax.broadcasted_iota(jnp.int32, (rows, rows), 1)
    return lax.rem(one, period) != lax.rem(two, period)


def attend_kernel(period, lead, qk_ref, v_ref, out_ref, acc_ref):
    rows, width = acc_ref.shape
    apart = tokens_apart(rows, period)
    queries, key_rows = qk_ref[0, :, :width], qk_ref[0, :, width : 2 * width]
    value_rows = v_ref[0, :, lead : lead + width]
    acc_ref[...] = jnp.zeros_like(acc_ref)
    for first, low, high in head_windows(width):
        mask = head_mask(first, low, high)
        probs = softmax_probs(queries[:, low:high] * mask, key_rows[:, low:high], apart)
        acc_ref[:, low:high] += jnp.dot(
            probs.astype(bf16), value_rows[:, low:high] * mask, preferred_element_type=f32
        )
    attended = acc_ref[...].astype(bf16)
    before = out_ref.shape[2] - width
    if before:
        attended = jnp.concatenate([jnp.zeros((rows, before), bf16), attended], axis=1)
    out_ref[0] = attended


def attend(qk, values, lead, width, before, period):
    blocks, rows = qk.shape[:2]

    def whole(cols):
        return pl.BlockSpec((1, rows, cols), lambda b: (b, 0, 0))

    return pl.pallas_call(
        partial(attend_kernel, period, lead),
        grid=(blocks,),
        out_shape=jax.ShapeDtypeStruct((blocks, rows, before + width), bf16),
        in_specs=[whole(qk.shape[2]), whole(values.shape[2])],
        out_specs=whole(before + width),
        scratch_shapes=[pltpu.VMEM((rows, width), f32)],
        compiler_params=pltpu.CompilerParams(vmem_limit_bytes=24 * MIB),
        cost_estimate=LIGHT,
        name="attend",
    )(qk, values)


def attend_grad_kernel(period, lead, skip, qk_ref, v_ref, da_ref, *refs):
    outs, sum_ref, (acc_q, acc_k, acc_v) = refs[:-4], refs[-4], refs[-3:]
    rows, width = acc_q.shape
    apart = tokens_apart(rows, period)
    queries, key_rows = qk_ref[0, :, :width], qk_ref[0, :, width : 2 * width]
    value_rows = v_ref[0, :, lead : lead + width]
    grad_att = da_ref[0, :, skip : skip + width]
    factor = HEAD_DIM ** (-0.5)
    for acc in (acc_q, acc_k, acc_v):
        acc[...] = jnp.zeros_like(acc)
    for first, low, high in head_windows(width):
        mask = head_mask(first, low, high)
        q_own = queries[:, low:high] * mask
        k_own = key_rows[:, low:high] * mask
        g_own = grad_att[:, low:high] * mask
        probs = softmax_probs(q_own, k_own, apart)
        grad_probs = row_dot(g_own, value_rows[:, low:high])
        inner = jnp.sum(grad_probs * probs, axis=-1, keepdims=True)
        grad_scores = (probs * (grad_probs - inner)).astype(bf16)
        acc_q[:, low:high] += jnp.dot(grad_scores, k_own, preferred_element_type=f32)
        acc_k[:, low:high] += col_dot(grad_scores, q_own)
        acc_v[:, low:high] += col_dot(probs.astype(bf16), g_own)
    grad_q = (acc_q[...] * factor).astype(bf16)
    outs[0][0, :, :width] = grad_q
    outs[0][0, :, width : 2 * width] = (acc_k[...] * factor).astype(bf16)
    grad_v = acc_v[...].astype(bf16)
    if len(outs) == 1:
        outs[0][0, :, 2 * width :] = grad_v
    else:
        outs[1][0] = jnp.concatenate([grad_v, jnp.zeros_like(grad_v)], axis=1)
    sum_ref[0, 0:1, :] = jnp.sum(grad_q.astype(f32), axis=0, keepdims=True)
    sum_ref[0, 1:2, :] = jnp.sum(grad_v.astype(f32), axis=0, keepdims=True)


def attend_grad(qk, values, lead, grad_att, skip, width, period):
    blocks, rows = qk.shape[:2]

    def whole(cols):
        return pl.BlockSpec((1, rows, cols), lambda b: (b, 0, 0))

    cols = [3 * width] if period else [2 * width, 2 * width]
    return pl.pallas_call(
        partial(attend_grad_kernel, period, lead, skip),
        grid=(blocks,),
        out_shape=[jax.ShapeDtypeStruct((blocks, rows, c), bf16) for c in cols]
        + [jax.ShapeDtypeStruct((blocks, 2, width), f32)],
        in_specs=[whole(qk.shape[2]), whole(values.shape[2]), whole(grad_att.shape[2])],
        out_specs=[whole(c) for c in cols] + [pl.BlockSpec((1, 2, width), lambda b: (b, 0, 0))],
        scratch_shapes=[pltpu.VMEM((rows, width), f32)] * 3,
        compiler_params=pltpu.CompilerParams(vmem_limit_bytes=24 * MIB),
        cost_estimate=LIGHT,
        name="attend_grad",
    )(qk, values, grad_att)


def on_chip():
    return pl.BlockSpec(memory_space=pltpu.VMEM)


def in_place():
    return pl.BlockSpec(memory_space=pl.ANY)


def call(kernel, name, inputs, streamed, outs, scratch=(), limit=24, out_specs=None):
    buffers = [pltpu.VMEM(w.shape, w.dtype) for w in streamed]
    sems = [pltpu.SemaphoreType.DMA((len(streamed),))] if streamed else []
    n_in, n_w, n_out = len(inputs), len(streamed), len(outs)

    def body(*refs):
        ins, away = refs[:n_in], refs[n_in : n_in + n_w]
        results = refs[n_in + n_w : n_in + n_w + n_out]
        rest = refs[n_in + n_w + n_out :]
        here, rest = rest[:n_w], rest[n_w:]
        copies = []
        if n_w:
            sem, rest = rest[0], rest[1:]
            copies = [pltpu.make_async_copy(a, h, sem.at[i]) for i, (a, h) in enumerate(zip(away, here))]
            for copy in copies:
                copy.start()

        def fetch(i):
            copies[i].wait()
            return here[i]

        kernel(ins, fetch, results, rest)

    return pl.pallas_call(
        body,
        out_shape=[jax.ShapeDtypeStruct(shape, dtype) for shape, dtype in outs],
        in_specs=[on_chip()] * n_in + [in_place()] * n_w,
        out_specs=out_specs or [on_chip()] * n_out,
        scratch_shapes=buffers + sems + list(scratch),
        compiler_params=pltpu.CompilerParams(vmem_limit_bytes=limit * MIB),
        cost_estimate=LIGHT,
        name=name,
    )(*inputs, *streamed)


def norm_parts(values):
    average = jnp.mean(values, axis=-1, keepdims=True)
    centered = values - average
    variance = jnp.mean(centered * centered, axis=-1, keepdims=True)
    inverse = lax.rsqrt(variance + EPSILON)
    return centered * inverse, inverse


def both(one, two):
    return jnp.concatenate([one[...], two[...]], axis=0)


def modulated(values, mods_ref, shift, scale):
    normed, _ = norm_parts(values)
    return (normed * (1.0 + mods_ref[scale : scale + 1, :]) + mods_ref[shift : shift + 1, :]).astype(bf16)


def norm_forward(x, mods, shift, scale):
    def kernel(ins, fetch, outs, scratch):
        outs[0][...] = modulated(ins[0][...], ins[1], shift, scale)

    return call(kernel, "norm_forward", [x, mods], [], [(x.shape, bf16)])[0]


def project_heads(normed, w_qk, w_vo, biases, row):
    rows, cols = 2 * normed[0].shape[0], w_qk.shape[1]

    def kernel(ins, fetch, outs, scratch):
        tokens = both(ins[0], ins[1])
        for i in range(2):
            bias = ins[2][row + i : row + i + 1, :]
            outs[i][...] = (jnp.dot(tokens, fetch(i)[...], preferred_element_type=f32) + bias).astype(bf16)

    return call(kernel, "project_heads", [*normed, biases], [w_qk, w_vo], [((rows, cols), bf16)] * 2)


def project_back(pairs, dtype, name):
    rows, cols = pairs[0][0].shape[0] // 2, pairs[0][1].shape[0]
    count = len(pairs)

    def kernel(ins, fetch, outs, scratch):
        out = row_dot(ins[0][...], fetch(0)[...])
        for i in range(1, count):
            out = out + row_dot(ins[i][...], fetch(i)[...])
        outs[0][...] = out[:rows]
        outs[1][...] = out[rows:].astype(dtype)

    return call(
        kernel, name, [p[0] for p in pairs], [p[1] for p in pairs], [((rows, cols), f32), ((rows, cols), dtype)]
    )


def residual(x, own, other, biases, bias_row, mods, gate, following):
    def kernel(ins, fetch, outs, scratch):
        branch = ins[1][...] + ins[2][...].astype(f32) + ins[3][bias_row : bias_row + 1, :]
        value = ins[0][...] + ins[4][gate : gate + 1, :] * branch
        outs[0][...] = branch
        outs[1][...] = value
        if following is None:
            outs[2][...] = value.astype(bf16)
        else:
            outs[2][...] = modulated(value, ins[4], *following)

    return call(
        kernel, "residual", [x, own, other, biases, mods], [], [(x.shape, f32), (x.shape, f32), (x.shape, bf16)]
    )


def gelu_parts(pre):
    inner = jnp.tanh(GELU_C * (pre + 0.044715 * (pre * pre * pre)))
    return inner


def mlp_forward(normed, up_a, up_b, down_a, down_b, biases, row, dtype):
    patches, cols = normed[0].shape[0], up_a.shape[1]
    model = down_a.shape[0]
    rows = 2 * patches

    def kernel(ins, fetch, outs, scratch):
        tokens = both(ins[0], ins[1])
        out = None
        for i in range(2):
            bias = ins[2][row + i : row + i + 1, :]
            pre = jnp.dot(tokens, fetch(2 * i)[...], preferred_element_type=f32) + bias
            outs[i][...] = pre
            hidden = (0.5 * pre * (1.0 + gelu_parts(pre))).astype(bf16)
            outs[2 + i][...] = hidden
            part = row_dot(hidden, fetch(2 * i + 1)[...])
            out = part if out is None else out + part
        outs[4][...] = out[:patches]
        outs[5][...] = out[patches:].astype(dtype)

    return call(
        kernel,
        "mlp_forward",
        [*normed, biases],
        [up_a, down_a, up_b, down_b],
        [((rows, cols), f32)] * 2 + [((rows, cols), bf16)] * 2 + [((patches, model), f32), ((patches, model), dtype)],
        limit=48,
    )


def mlp_up(normed, up_a, up_b, biases, row):
    rows, cols = 2 * normed[0].shape[0], up_a.shape[1]

    def kernel(ins, fetch, outs, scratch):
        tokens = both(ins[0], ins[1])
        for i in range(2):
            bias = ins[2][row + i : row + i + 1, :]
            pre = jnp.dot(tokens, fetch(i)[...], preferred_element_type=f32) + bias
            outs[i][...] = pre
            outs[2 + i][...] = (0.5 * pre * (1.0 + gelu_parts(pre))).astype(bf16)

    return call(
        kernel,
        "mlp_up",
        [*normed, biases],
        [up_a, up_b],
        [((rows, cols), f32)] * 2 + [((rows, cols), bf16)] * 2,
        limit=32,
    )


def mlp_backward(grad, pre, up, down, so_far):
    patches, model = grad[0].shape
    rows, cols = pre.shape
    last = so_far is not None

    def kernel(ins, fetch, outs, scratch):
        tokens = both(ins[0], ins[1])
        grad_hidden = jnp.dot(tokens, fetch(0)[...], preferred_element_type=f32)
        value = fetch(1)[...]
        inner = gelu_parts(value)
        slope = 0.5 * (1.0 + inner) + 0.5 * value * (1.0 - inner * inner) * (
            GELU_C * (1.0 + 3.0 * 0.044715 * (value * value))
        )
        grad_pre = (grad_hidden * slope).astype(bf16)
        outs[0][...] = grad_pre
        outs[1][0:1, :] = jnp.sum(grad_pre.astype(f32), axis=0, keepdims=True)
        outs[1][1:2, :] = jnp.sum(tokens.astype(f32), axis=0, keepdims=True)
        out = row_dot(grad_pre, fetch(2)[...])
        if last:
            out = out + fetch(3)[...]
            outs[2][...] = out[:patches]
            outs[3][...] = out[patches:].astype(bf16)
        else:
            outs[2][...] = out

    tail = [((patches, model), f32), ((patches, model), bf16)] if last else [((rows, model), f32)]
    return call(
        kernel,
        "mlp_backward",
        list(grad),
        [down, pre, up] + ([so_far] if last else []),
        [((rows, cols), bf16), ((2, cols), f32)] + tail,
        limit=32,
    )


def grad_heads(grad, w_vo):
    patches, model = grad[0].shape
    cols = w_vo.shape[1]

    def kernel(ins, fetch, outs, scratch):
        tokens = both(ins[0], ins[1])
        outs[1][...] = jnp.sum(tokens.astype(f32), axis=0, keepdims=True)
        outs[0][...] = jnp.dot(tokens, fetch(0)[...], preferred_element_type=f32).astype(bf16)

    return call(kernel, "grad_heads", list(grad), [w_vo], [((2 * patches, cols), bf16), ((1, model), f32)])


def norm_backward(g, own, other, x, mods, scale, gate, branch):
    rows, model = x.shape

    def kernel(ins, fetch, outs, scratch):
        grad = ins[1][...] + ins[2][...].astype(f32)
        normed, inverse = norm_parts(ins[3][...])
        scaled = grad * (1.0 + ins[4][scale : scale + 1, :])
        mean_one = jnp.mean(scaled, axis=-1, keepdims=True)
        mean_two = jnp.mean(scaled * normed, axis=-1, keepdims=True)
        value = ins[0][...] + inverse * (scaled - mean_one - normed * mean_two)
        outs[0][...] = value
        outs[1][0:1, :] = jnp.sum(grad, axis=0, keepdims=True)
        outs[1][1:2, :] = jnp.sum(grad * normed, axis=0, keepdims=True)
        if gate is not None:
            outs[1][2:3, :] = jnp.sum(value * ins[5][...], axis=0, keepdims=True)
            outs[2][...] = (ins[4][gate : gate + 1, :] * value).astype(bf16)

    inputs = [g, own, other, x, mods] + ([] if gate is None else [branch])
    outs = [(x.shape, f32), ((3, model), f32)] + ([] if gate is None else [(x.shape, bf16)])
    return call(kernel, "norm_backward", inputs, [], outs)


def insert_bit(rest, bit):
    low = rest & ((1 << bit) - 1)
    return (rest - low) * 2 + low


def weight_grad(pairs, bit, name):
    clusters, parts = lax.axis_size("dp"), lax.axis_size("seq")
    model, cols = pairs[0][0].shape[1], pairs[0][1].shape[1]
    rows = model // (clusters * parts)
    mine = ((lax.axis_index("seq") >> bit) & 1).astype(jnp.int32).reshape(1)
    shape = (clusters, parts // 2, rows, cols)
    count = len(pairs)

    def body(mine_ref, *refs):
        ins, outs, (whole, sem) = refs[: 2 * count], refs[2 * count : 2 * count + 2], refs[2 * count + 2 :]
        out = col_dot(ins[0][...], ins[1][...])
        for i in range(1, count):
            out = out + col_dot(ins[2 * i][...], ins[2 * i + 1][...])
        copies = []
        for c in range(clusters):
            for part in range(parts):
                at = (c * parts + part) * rows
                whole[c * parts + part] = out[at : at + rows].astype(bf16)
        for c in range(clusters):
            for rest in range(parts // 2):
                start = c * parts + insert_bit(rest, bit)
                for which in range(2):
                    side = mine_ref[0] if which == 0 else 1 - mine_ref[0]
                    copy = pltpu.make_async_copy(
                        whole.at[start + (side << bit)],
                        outs[which].at[c, rest],
                        sem.at[(c * (parts // 2) + rest) * 2 + which],
                    )
                    copy.start()
                    copies.append(copy)
        for copy in copies:
            copy.wait()

    return pl.pallas_call(
        body,
        out_shape=[jax.ShapeDtypeStruct(shape, bf16)] * 2,
        in_specs=[pl.BlockSpec(memory_space=pltpu.SMEM)] + [on_chip()] * (2 * count),
        out_specs=[in_place()] * 2,
        scratch_shapes=[
            pltpu.VMEM((clusters * parts, rows, cols), bf16),
            pltpu.SemaphoreType.DMA((clusters * parts,)),
        ],
        compiler_params=pltpu.CompilerParams(vmem_limit_bytes=32 * MIB),
        cost_estimate=LIGHT,
        name=name,
    )(mine, *[array for pair in pairs for array in pair])


def with_other(flow, own):
    flow.now += SWAP
    return own, swap(own)


def dispatch_in(flow, arrays, cost, hold):
    arrays[0] = flow.step(2.0, arrays[0])
    if hold:
        flow.hold(cost)
        result = dispatch(arrays)
        flow.release(result)
        return result
    flow.now += 2.5 * cost
    return dispatch(arrays)


def collect_in(flow, rows, cuts, cost, hold):
    rows = flow.step(2.0, rows)
    if hold:
        flow.hold(cost)
        result = collect(rows, cuts)
        flow.release(result[0])
        return result
    flow.now += 2.5 * cost
    return collect(rows, cuts)


def layer_forward(flow, x, normed_one, mods, layer, units, biases_of, temporal, following):
    attention_unit, mlp_unit = units
    patches = x.shape[0]
    base = 6 * layer
    normed_one = with_other(flow, normed_one)
    w_qk, w_vo = attention_unit()
    width = w_qk.shape[1] // 2
    biases = biases_of()
    qk, vo = flow.ran(project_heads((flow.step(6.5, normed_one[0]), normed_one[1]), w_qk, w_vo, biases, base))
    qk = qk.reshape(2, patches, -1)
    vo = vo.reshape(2, patches, -1)
    if temporal:
        period = patches // lax.axis_size("seq")
        qkv = dispatch_in(flow, [qk, vo[:, :, :width]], 17.0 * TRIP, False)
        heads = (flow.step(3.5, qkv), qkv, 2 * width)
        attended = attend(*heads, width, 0, period)
        attended = collect_in(flow, attended, ((0, period, 0, width, width, 0),), 11.0 * TRIP, False)[0]
    else:
        heads = (flow.step(3.5, qk), vo, 0)
        attended = attend(*heads, width, width, None).reshape(2 * patches, -1)
    own, other = flow.ran(project_back([(flow.step(2.5, attended), w_vo)], f32, "project_out"))
    other = swap(other)
    flow.now += SWAP
    branch, x_mid, normed_two = flow.ran(
        residual(x, flow.step(2.0, own), other, biases, base + 2, mods, base + 2, (base + 3, base + 4))
    )
    normed_two = with_other(flow, normed_two)
    if following is not None:
        w_up_a, w_down_a, w_up_b, w_down_b = mlp_unit()
        tokens = (flow.step(11.0, normed_two[0]), normed_two[1])
        pre_a, pre_b, hidden_a, hidden_b, own, other = flow.ran(
            mlp_forward(tokens, w_up_a, w_up_b, w_down_a, w_down_b, biases, base + 3, f32)
        )
        other = swap(other)
        flow.now += SWAP
        mlp, x_next, after = flow.ran(
            residual(x_mid, flow.step(2.0, own), other, biases, base + 5, mods, base + 5, following)
        )
        finish = None
        downs = (w_down_a, w_down_b)
    else:
        w_up_a, w_down_a, w_up_b, w_down_b = mlp_unit()
        tokens = (flow.step(8.0, normed_two[0]), normed_two[1])
        pre_a, pre_b, hidden_a, hidden_b = flow.ran(mlp_up(tokens, w_up_a, w_up_b, biases, base + 3))
        downs = (w_down_a, w_down_b)
        mlp = x_next = after = None

        def finish(down_a, down_b):
            first = flow.step(4.0, hidden_a)
            own, other = flow.ran(project_back([(first, down_a), (hidden_b, down_b)], f32, "project_down"))
            other = swap(other)

            def rest():
                return flow.ran(residual(x_mid, flow.step(2.0, own), other, biases, base + 5, mods, base + 5, None))

            return rest

    saved = (x, normed_one, heads, attended, branch, x_mid, normed_two, pre_a, pre_b, hidden_a, hidden_b, mlp)
    weights = (w_qk, w_vo, w_up_a, w_up_b, downs)
    return x_next, after, saved, weights, finish


def layer_backward(flow, g, grad_mlp, mods, layer, weights, saved, temporal, below, finish):
    w_qk, w_vo, w_up_a, w_up_b, downs = weights
    x, normed_one, heads, attended, branch, x_mid, normed_two, pre_a, pre_b, hidden_a, hidden_b, _ = saved
    patches = x.shape[0]
    width = w_qk.shape[1] // 2
    base = 6 * layer
    done = [Scatter(flow, 20 - 4 * layer - unit) for unit in range(3)]
    bits = (bits_of(lax.axis_size("seq")) - 1, 0)

    def reduce_half(unit, which, pairs, name):
        first = flow.step(5.0, pairs[0][1])
        done[unit].give(which, *flow.ran(weight_grad([(pairs[0][0], first)] + pairs[1:], bits[which], name)))

    def joined(pair):
        return jnp.concatenate(pair, axis=0)

    grad_mlp = with_other(flow, grad_mlp)
    grad_mlp_rows = joined(grad_mlp)
    reduce_half(2, 0, [(grad_mlp_rows, hidden_a)], "down_grad")
    reduce_half(2, 1, [(grad_mlp_rows, hidden_b)], "down_grad")
    w_down_a, w_down_b = downs
    normed_rows = joined(normed_two)
    tokens = (flow.step(7.0, grad_mlp[0]), grad_mlp[1])
    grad_pre_a, sums_a, so_far = flow.ran(mlp_backward(tokens, pre_a, w_up_a, w_down_a, None))
    reduce_half(1, 0, [(normed_rows, grad_pre_a)], "up_grad")
    tokens = (flow.step(8.0, grad_mlp[0]), grad_mlp[1])
    grad_pre_b, sums_b, own, other = flow.ran(mlp_backward(tokens, pre_b, w_up_b, w_down_b, so_far))
    other = swap(other)
    reduce_half(1, 1, [(normed_rows, grad_pre_b)], "up_grad")
    g_mid, sums_two, grad_branch = flow.ran(
        norm_backward(g, flow.step(2.0, own), other, x_mid, mods, base + 4, base + 2, branch)
    )
    other_branch = swap(grad_branch)
    flow.now += 4.0
    grad_branch = (flow.step(2.5, grad_branch), other_branch)
    grad_att, sum_branch = flow.ran(grad_heads(grad_branch, w_vo))
    grad_att = grad_att.reshape(2, patches, -1)
    rest = finished = None
    if finish is not None:
        rest = finish(w_down_a, w_down_b)
    if temporal:
        period = patches // lax.axis_size("seq")
        grad_att = dispatch_in(flow, [grad_att[:, :, width:]], 10.0 * TRIP, HOLD)
        grad_qkv, sums_pair = flow.ran(attend_grad(*heads, flow.step(10.5, grad_att), 0, width, period))
        cuts = ((0, period, 0, 2 * width, 0, 0), (0, period, 2 * width, width, 0, width))
        grad_qk, grad_v = collect_in(flow, grad_qkv, cuts, 18.0 * TRIP, HOLD)
    else:
        grad_qk, grad_v, sums_pair = flow.ran(
            attend_grad(*heads, flow.step(10.5, grad_att), width, width, None)
        )
        grad_qk = grad_qk.reshape(2 * patches, -1)
        grad_v = grad_v.reshape(2 * patches, -1)
    if rest is not None:
        finished = rest()
    own, other = flow.ran(
        project_back([(flow.step(5.0, grad_qk), w_qk), (grad_v, w_vo)], bf16, "grad_normed")
    )
    other = swap(other)
    rows_one = joined(normed_one)
    reduce_half(0, 0, [(rows_one, grad_qk)], "heads_grad")
    own = flow.step(2.0, own)
    if below is None:
        g_below, sums_one = flow.ran(norm_backward(g_mid, own, other, x, mods, base + 1, None, None))
        grad_below = None
    else:
        g_below, sums_one, grad_below = flow.ran(
            norm_backward(g_mid, own, other, x, mods, base + 1, base - 1, below)
        )
    reduce_half(0, 1, [(rows_one, grad_v), (joined(grad_branch), attended)], "heads_grad")
    mod_sums = [sums_one[0], sums_one[1], sums_two[2], sums_two[0], sums_two[1]]
    bias_sums = [
        jnp.sum(sums_pair, axis=0).reshape(-1),
        sum_branch.reshape(-1),
        sums_a[0],
        sums_b[0],
        sums_a[1],
    ]
    return g_below, grad_below, mod_sums, sums_one[2], bias_sums, done, finished


def shards(
    tokens,
    conditioning,
    cotangent,
    modulation_weight,
    modulation_bias,
    triple_weight,
    pair_bias,
    out_weight,
    out_bias,
    hidden_weight,
    hidden_bias,
    output_weight,
    output_bias,
):
    layers, _, _, width = triple_weight.shape
    model = tokens.shape[3]
    patches = tokens.shape[2]
    own_clips = tokens.shape[0] // lax.axis_size("tensor")
    all_clips = conditioning.shape[0]
    assert own_clips == 1 and tokens.shape[1] == 1 and layers == 2
    assert model == 2 * width and hidden_weight.shape[2] == 2 * model
    units = hidden_weight.shape[2]
    half = units // 2
    dp_index, seq_index = lax.axis_index("dp"), lax.axis_index("seq")
    core = lax.axis_index("tensor")
    n_dp, n_seq, n_core = lax.axis_size("dp"), lax.axis_size("seq"), lax.axis_size("tensor")

    packed = jnp.concatenate(
        [pair_bias.reshape(layers, -1), out_bias, hidden_bias.reshape(layers, -1), output_bias], axis=1
    ).reshape(-1)
    rows = triple_weight.shape[1]

    def attention_unit(layer):
        triple = triple_weight[layer]
        first = jnp.concatenate([triple[:, 0], triple[:, 1]], axis=1)
        second = jnp.concatenate([triple[:, 2], out_weight[layer].T], axis=1)
        if layer == 0:
            extra = jnp.zeros((8 * 2 * width,), bf16).at[: packed.shape[0]].set(packed).reshape(8, -1)
            first = jnp.concatenate([first, extra])
            second = jnp.concatenate([second, jnp.zeros_like(extra)])
        return first, second

    def mlp_unit(layer):
        down = output_weight[layer].T
        up = hidden_weight[layer]
        parts = (slice(0, half), slice(half, None))
        return [[jnp.concatenate([up[:, part], down[:, part]], axis=1) for part in parts]]

    flow = Flow()
    flow.now = 8.0
    gathers = []
    for layer in range(layers):
        whole = (0, rows, 0, 2 * width, 0, 0)
        first_cuts = (whole, (rows, 8, 0, 2 * width, 0, 0)) if layer == 0 else (whole,)
        attention = Gather(flow, 2 * layer, attention_unit(layer), dp_index, seq_index, (first_cuts, (whole,)), 2.0)
        pair_cuts = ((0, rows, 0, half, 0, 0), (0, rows, half, half, 0, 0))
        mlp = mlp_unit(layer)
        mlp_cuts = (pair_cuts, pair_cuts) if len(mlp) == 1 else ((whole,), (whole,))
        mlp = [
            Gather(flow, 2 * layer + 1 + i, halves, dp_index, seq_index, mlp_cuts, 3.5 if len(mlp) == 1 else 2.0)
            for i, halves in enumerate(mlp)
        ]
        gathers.append((attention, mlp))

    act_cond, silu_back = jax.vjp(jax.nn.silu, conditioning)
    act_low = act_cond.astype(bf16)
    local_term = jnp.einsum("cd,lde->cle", act_low, modulation_weight, preferred_element_type=f32)
    bias_cols = modulation_bias.shape[1]
    offset = ((dp_index * n_seq + seq_index) * n_core + core) * bias_cols
    bias_full = lax.dynamic_update_slice(
        jnp.zeros((layers, local_term.shape[2]), f32), modulation_bias.astype(f32), (jnp.int32(0), offset)
    )
    contribution = (local_term + bias_full[None]).reshape(n_dp, n_core, -1)
    contribution = take(contribution, 1, core) + swap(take(contribution, 1, 1 - core))
    contribution = flow.step(25.0, contribution)
    mods = sum_small(scatter_small(contribution, "dp"), "seq").reshape(layers * 6, model)

    def unpack(spread):
        spread = spread.reshape(n_dp * n_seq, -1)[:, : packed.shape[0]].reshape(n_dp * n_seq, layers, -1)
        spread = spread.transpose(1, 0, 2).astype(f32)
        cuts, at = [], 0
        for size in (pair_bias.shape[3], pair_bias.shape[3], out_bias.shape[1], hidden_bias.shape[2], output_bias.shape[1]):
            cuts.append(spread[:, :, at : at + size].reshape(layers, -1))
            at += size
        blank = jnp.zeros_like(cuts[0])
        return jnp.concatenate([cuts[0], blank, cuts[1], blank, *cuts[2:]], axis=1).reshape(6 * layers, model)

    found = {}

    def attention_weights(layer):
        first, second = gathers[layer][0].result()
        if layer == 0:
            found["biases"] = unpack(first[1])
        return first[0], second[0]

    def mlp_weights(layer):
        first, second = gathers[layer][1][0].result()
        return first + second

    x = take(tokens, 0, core).reshape(patches, model).astype(f32)
    after = norm_forward(x, mods, 0, 1)
    kept, weights = [], []
    for layer in range(layers):
        following = (6 * layer + 6, 6 * layer + 7) if layer + 1 < layers else None
        pending = (partial(attention_weights, layer), partial(mlp_weights, layer))
        x, after, saved, layer_weights, finish = layer_forward(
            flow, x, after, mods, layer, pending, lambda: found["biases"], layer == 1, following
        )
        kept.append(saved)
        weights.append(layer_weights)

    def to_both(own):
        other = swap(own)
        pair = jnp.stack([jnp.where(core == 0, own, other), jnp.where(core == 0, other, own)])
        return pair.reshape((2, 1) + own.shape)

    g = take(cotangent, 0, core).reshape(patches, model).astype(f32)
    grad_mlp = (mods[6 * layers - 1] * g).astype(bf16)
    grad_gates = [None] * layers
    top = g
    mod_grads, bias_grads, done = [None] * layers, [None] * layers, [None] * layers
    flow.depth, flow.scale = DEPTH, SCALE_B
    for layer in reversed(range(layers)):
        below = kept[layer - 1][-1] if layer else None
        g, grad_mlp, mod_sums, grad_gate, bias_grads[layer], done[layer], finished = layer_backward(
            flow, g, grad_mlp, mods, layer, weights[layer], kept[layer], layer == 1, below, finish
        )
        if finished is not None:
            grad_gates[layer] = jnp.sum(top * finished[0], axis=0)
            activations = to_both(finished[2])
            finish = None
        mod_grads[layer] = jnp.concatenate(mod_sums + [grad_gates[layer]])
        if layer:
            grad_gates[layer - 1] = grad_gate
    input_grad = to_both(g)
    flow.until(lambda: all(unit.total is not None for layer in range(layers) for unit in done[layer]))

    def stack_layers(which, build):
        return jnp.stack([build(done[layer][which].total) for layer in range(layers)])

    triple_grad = stack_layers(
        0, lambda u: jnp.stack([u[0][:, :width], u[0][:, width:], u[1][:, :width]], axis=1)
    )
    out_grad = stack_layers(0, lambda u: u[1][:, width:].T)
    hidden_grad = stack_layers(1, lambda u: jnp.concatenate([u[0], u[1]], axis=1))
    output_grad = stack_layers(2, lambda u: jnp.concatenate([u[0], u[1]], axis=1).T)

    flat = [part for layer in range(layers) for part in bias_grads[layer]]
    summed = sum_small(jnp.concatenate(mod_grads + flat), "seq").astype(bf16)
    mods_size = 6 * model * layers
    pair = jnp.concatenate([summed[:mods_size], swap(summed[:mods_size]), summed[mods_size:]])
    spread = gather_small(pair.reshape(1, -1, 128), "dp").reshape(n_dp, -1)
    spread = [spread[rel] for rel in range(n_dp)]
    grad_mods = jnp.stack([s[c * mods_size : (c + 1) * mods_size] for s in spread for c in range(n_core)])
    grad_mods = grad_mods.reshape(all_clips, layers, -1)
    clip = jnp.arange(all_clips)
    clip = (clip // n_core ^ dp_index) * n_core + (clip % n_core ^ core)
    bias_sums = add_up([s[n_core * mods_size :] for s in spread]).reshape(layers, -1)
    owner = dp_index * n_seq + seq_index
    bias_out, at = [], 0
    for size, shape in (
        (width, None),
        (width, None),
        (model, out_bias.shape),
        (units, hidden_bias.shape),
        (model, output_bias.shape),
    ):
        part = bias_sums[:, at : at + size].reshape(layers, n_dp * n_seq, -1)
        part = take(part, 1, owner)
        bias_out.append(part if shape is None else part.reshape(shape))
        at += size
    pair_out = jnp.stack(bias_out[:2], axis=1).reshape(pair_bias.shape)
    out_bias_grad, hidden_bias_grad, output_bias_grad = bias_out[2:]
    modulation_weight_grad = jnp.einsum("cd,cle->lde", act_low[clip], grad_mods, preferred_element_type=f32)
    modulation_bias_grad = lax.dynamic_slice_in_dim(
        jnp.sum(grad_mods, axis=0, dtype=f32), offset, bias_cols, 1
    )
    grad_act = jnp.einsum("cle,lde->cd", grad_mods, modulation_weight, preferred_element_type=f32)
    cond_grad = silu_back(grad_act[clip])[0]
    return (
        activations,
        input_grad,
        cond_grad,
        modulation_weight_grad,
        modulation_bias_grad,
        triple_grad,
        pair_out,
        out_grad,
        out_bias_grad,
        hidden_grad,
        hidden_bias_grad,
        output_grad,
        output_bias_grad,
    )


def solution(mesh):
    owners = ("dp", "seq")
    everyone = ("dp", "seq", "tensor")
    rows = P("dp", "seq", None, None)
    weights = (
        P(None, everyone, None),
        P(None, everyone),
        P(None, owners, None, "tensor"),
        P(None, None, "tensor", owners),
        P(None, "tensor", owners),
        P(None, owners),
        P(None, owners, "tensor"),
        P(None, "tensor", owners),
        P(None, "tensor", owners),
        P(None, owners),
    )
    return jax.shard_map(
        shards,
        mesh=mesh,
        in_specs=(rows, P(None, everyone), rows) + weights,
        out_specs=(rows, rows, P(None, everyone)) + weights,
        check_vma=False,
    )
```
